32 devices in a mesh: plan: 16 (over z, x, core), layer: 2 (over y).
Axes of the slice: x: 2, y: 2, z: 4, core: 2. Of those that a mesh axis runs over, the one named last changes fastest.
Arguments:
- dual_block: float32 [2, 16, 1024, 1024], P('layer', 'plan'), may hold values from -1 to 6, as said below
- start: float32 [2, 16, 8, 1024], P('layer', 'plan'), may hold values from -6 to 6
- load: float32 [2, 16, 8, 1024], P('layer', 'plan'), may hold values from -40 to 40
- partners: int32 [16, 6], P('plan'), may hold values from 0 to 15, as said below
- jump_rows: int32 [2, 16, 6, 32], P('layer', 'plan'), may hold values from 128 to 895, as said below
- counts: int32 [2, 16, 6], P('layer', 'plan'), may hold values from 16 to 32, as said below
- contact: int32 [2, 16, 1024], P('layer', 'plan'), may hold values 0 or 1
Outputs:
- multipliers: float32 [2, 16, 8, 1024], P('layer', 'plan')
- gradient: float32 [2, 16, 8, 1024], P('layer', 'plan')
The draws below stay inside these ranges and needn't reach their ends.
Inputs may be any that keep to these rules, and one draw needn't show every extreme that they name: `dual_block`: every block is symmetric positive definite. In every round the partners form a perfect matching of the 16 subdomains with nobody paired to itself, and no pair meets in two rounds. `jump_rows`: the 192 rows of one subdomain are distinct and lie outside its first and last 128 rows; row k of a subdomain's block for round r meets row k of its partner's block. `counts`: both partners of a round have the same count; rows at position count or beyond are padding; every count of round 0 is 32.
All inputs are finite; a program needn't handle non-finite values. No bound on the sum of `contact` on one device may be relied on, other than what follows from the above.
Results may differ from the reference program's by a relative error of at most 0.0001.
Values sent between devices are 32-bit elements; how exact they have to be, the bound alone decides.
A program may use at most 64 MiB of HBM per device.

```python
import jax
import jax.numpy as jnp
from jax import lax

M = 1024
LOADS = 8
FACE = 128
JR = 32
ROUNDS = 6
ITERS = 4
PLANS = 16
LAYERS = 2


def matching_table(key):
    relabel = jax.random.permutation(jax.random.fold_in(key, 11), PLANS).astype(jnp.int32)
    chosen = jax.random.permutation(jax.random.fold_in(key, 12), PLANS - 1)[:ROUNDS].astype(jnp.int32)
    inverse = jnp.argsort(relabel, stable=True).astype(jnp.int32)
    slots = inverse[:, None]
    pivot = chosen[None, :]
    mirror = jnp.mod(2 * pivot - slots, PLANS - 1)
    position = jnp.where(slots == PLANS - 1, pivot, jnp.where(slots == pivot, PLANS - 1, mirror))
    return relabel[position].astype(jnp.int32)


def draw_partners(key, part):
    return matching_table(key)


def draw_counts(key, part):
    partner_ids = matching_table(key)
    lower = jnp.minimum(jnp.arange(PLANS, dtype=jnp.int32)[:, None], partner_ids)
    drawn = jax.random.randint(jax.random.fold_in(key, 13), (LAYERS, ROUNDS, PLANS), JR // 2, JR + 1)
    picked = drawn[:, jnp.arange(ROUNDS)[None, :], lower]
    return picked.at[:, :, 0].set(JR).astype(jnp.int32)


def draw_jump_rows(key, part):
    keys = jax.random.split(jax.random.fold_in(key, 14), LAYERS * PLANS)
    chosen = jax.vmap(lambda one_key: jax.random.permutation(one_key, M - 2 * FACE)[:ROUNDS * JR])(keys)
    return (chosen + FACE).reshape(LAYERS, PLANS, ROUNDS, JR).astype(jnp.int32)


def draw_dual_block(key, part):
    normal_part = jax.random.normal(jax.random.fold_in(key, 21), (LAYERS, PLANS, M, M), jnp.float32)
    symmetric = (normal_part + jnp.swapaxes(normal_part, 2, 3)) / jnp.sqrt(2.0)
    off_scale = 0.7
    diagonal = jax.random.uniform(jax.random.fold_in(key, 22), (LAYERS, PLANS, M), jnp.float32, 2.0, 4.0)
    identity = jnp.eye(M, dtype=jnp.float32)
    off_diag = symmetric * (off_scale / jnp.sqrt(1.0 * M)) * (1.0 - identity)
    return off_diag + diagonal[:, :, :, None] * identity


def draw_load(key, part):
    depth = jnp.arange(LAYERS, dtype=jnp.float32) / max(LAYERS - 1, 1)
    ramp = (1.0 + 2.0 * depth)[:, None, None, None]
    values = jnp.clip(jax.random.normal(jax.random.fold_in(key, 31), (LAYERS, PLANS, LOADS, M), jnp.float32), -4.0, 4.0)
    return values * ramp


def touch_ends(result, key, smallest, top_value):
    place = [jax.random.randint(jax.random.fold_in(key, axis), (), 0, length) for axis, length in enumerate(result.shape)]
    widest = result.shape.index(max(result.shape))
    beside = place[:widest] + [(place[widest] + 1) % result.shape[widest]] + place[widest + 1:]
    return result.at[tuple(place)].set(smallest).at[tuple(beside)].set(top_value)


def levels(key, dims, cuts, low, high):
    gain = 1.0
    for axis_at, blocks in cuts:
        steps = jax.random.uniform(jax.random.fold_in(jax.random.fold_in(key, 6), axis_at), (blocks,), jnp.float32, low / len(cuts), high / len(cuts))
        gain = gain * jnp.repeat(jnp.exp(steps), dims[axis_at] // blocks).reshape((-1,) + (1,) * (len(dims) - 1 - axis_at))
    return gain


def scatter_about(rng, dims, scale, most, shards=(), held_as=jnp.bfloat16):
    entries = jax.random.normal(rng, dims, jnp.float32) * scale
    if len(shards) > 0:
        entries = levels(rng, dims, shards, -0.22, 0.18) * entries
    return jnp.clip(entries, min=-most, max=most).astype(held_as)


def setup_inputs(seed: int = 0) -> dict:
    arg_keys = jax.random.split(jax.random.key(seed), 8)
    return {
        "dual_block": draw_dual_block(jax.random.fold_in(arg_keys[7], 71), 0),
        "start": scatter_about(arg_keys[1], (LAYERS, PLANS, LOADS, M), 1.0, 6.0, ((0, 2), (1, 16)), jnp.float32),
        "load": draw_load(jax.random.fold_in(arg_keys[7], 71), 0),
        "partners": draw_partners(jax.random.fold_in(arg_keys[7], 71), 0),
        "jump_rows": draw_jump_rows(jax.random.fold_in(arg_keys[7], 71), 0),
        "counts": draw_counts(jax.random.fold_in(arg_keys[7], 71), 0),
        "contact": touch_ends((jax.random.randint(arg_keys[6], (LAYERS, PLANS, M), 0, 2) < 1).astype(jnp.int32), jax.random.fold_in(arg_keys[6], 1), 0, 1),
    }


highest = lax.Precision.HIGHEST
coupling = 1.0


def add_rows(total, indices, values):
    return total.at[:, indices].add(values)


def apply_dual(field, dual_block, partners, jump_rows, valid_mask):
    local_term = jnp.einsum("lpnm,lpmk->lpnk", field, dual_block, precision=highest)
    layer_count, plan_count, load_count, width = field.shape
    zeros_edge = jnp.zeros_like(field[:1, :, :, :FACE])
    from_below = jnp.concatenate([zeros_edge, field[:-1, :, :, width - FACE:]], axis=0)
    from_above = jnp.concatenate([field[1:, :, :, :FACE], zeros_edge], axis=0)
    middle = jnp.zeros((layer_count, plan_count, load_count, width - 2 * FACE), jnp.float32)
    neighbour = jnp.concatenate([from_below, middle, from_above], axis=3)
    positions = jnp.arange(width)
    edge_mask = (positions < FACE) | (positions >= width - FACE)
    face_term = jnp.where(edge_mask, field, 0.0) - neighbour
    flat_rows = jump_rows.reshape(layer_count, plan_count, 1, ROUNDS * JR).astype(jnp.int32)
    flat_rows = jnp.broadcast_to(flat_rows, (layer_count, plan_count, load_count, ROUNDS * JR))
    gathered = jnp.take_along_axis(field, flat_rows, axis=3).reshape(layer_count, plan_count, load_count, ROUNDS, JR)
    partner_vals = jnp.stack(
        [jnp.take(gathered[:, :, :, r, :], partners[:, r].astype(jnp.int32), axis=1) for r in range(ROUNDS)],
        axis=3)
    jump_diff = (gathered - partner_vals) * valid_mask[:, :, None, :, :]
    jump_term = jax.vmap(jax.vmap(add_rows))(
        jnp.zeros_like(field),
        jump_rows.reshape(layer_count, plan_count, ROUNDS * JR).astype(jnp.int32),
        jump_diff.reshape(layer_count, plan_count, load_count, ROUNDS * JR))
    return local_term + coupling * (face_term + jump_term)


def reference(dual_block, start, load, partners, jump_rows, counts, contact):
    valid_mask = (jnp.arange(JR)[None, None, None, :] < counts[:, :, :, None]).astype(jnp.float32)
    is_contact = (contact == 1)[:, :, None, :]
    multipliers = start
    gradient = start
    for iteration in range(ITERS):
        gradient = apply_dual(multipliers, dual_block, partners, jump_rows, valid_mask) - load
        image = apply_dual(gradient, dual_block, partners, jump_rows, valid_mask)
        grad_sq = jnp.sum(gradient * gradient, axis=(0, 1, 3))
        curvature = jnp.sum(gradient * image, axis=(0, 1, 3))
        step_size = (grad_sq + 1e-6) / (curvature + 1e-6)
        moved = multipliers - step_size[None, None, :, None] * gradient
        multipliers = jnp.where(is_contact, jnp.maximum(moved, 0.0), moved)
    return multipliers, gradient
```

```python
import functools

import jax
import jax.numpy as jnp
from jax import lax
from jax.experimental import pallas as pl
from jax.experimental.pallas import tpu as pltpu
from jax.sharding import PartitionSpec as P

FACE = 128
ITERS = 4
PLANES = 4
CHUNK = 256
MESH = pl.DeviceIdType.MESH
F32 = jnp.float32
BF16 = jnp.bfloat16


def split2(x):
    hi = x.astype(BF16)
    lo = (x - hi.astype(F32)).astype(BF16)
    return jnp.concatenate([hi, lo], axis=0)


def split3(x):
    hi = x.astype(BF16)
    rest = x - hi.astype(F32)
    mid = rest.astype(BF16)
    lo = (rest - mid.astype(F32)).astype(BF16)
    return jnp.concatenate([hi, mid, lo], axis=0)


def fold(y, parts):
    n = y.shape[0] // parts
    total = y[:n]
    for i in range(1, parts):
        total = total + y[i * n : (i + 1) * n]
    return total


def kernel(
    plans, layers, block_hbm, start_hbm, load_hbm, partners_hbm, rows_hbm, counts_hbm, contact_hbm,
    out_ref,
    start_ref, load_ref, partners_ref, rows_ref, counts_ref, contact_ref,
    block_f32, block_hi, block_lo, select, front_hi, front_lo,
    init_send, send_rows, init_rows, recv_rows, init_face, recv_face, meet, fcon_send, fcon_recv, ar_send, ar_recv,
    products, m_rows, h_rows, h_con, own_con, h_face, load_rows, face_send,
    small_sem, block_sem, rows_send_sem, init_rows_sem, rows_recv_sem, init_face_sem, meet_send_sem, meet_sem,
    face_send_sem, face_recv_sem, fcon_send_sem, fcon_recv_sem, ar_send_sem, ar_recv_sem,
    init_send_sem, init_face_send_sem,
):
    out_m, out_g = out_ref.at[pl.ds(0, 1)], out_ref.at[pl.ds(1, 1)]
    rounds, jr = rows_ref.shape[0], rows_ref.shape[2]
    loads, width = start_ref.shape[2], start_ref.shape[3]
    lanes = plans * jr
    per = 128 // jr
    halves = loads // per
    tiles = lanes // 128
    total = plans * layers
    part_of = plans // PLANES
    plan = lax.axis_index("plan")
    layer = lax.axis_index("layer")
    me = plan * layers + layer

    plane = plan // part_of
    place = lax.rem(plan, part_of)
    side = 1 - 2 * ((2 * plan) // plans)
    barrier = pltpu.get_barrier_semaphore()

    def greet(o, c):
        d = lax.rem(me + o, total)
        pl.semaphore_signal(
            barrier, inc=1, device_id={"plan": d // layers, "layer": lax.rem(d, layers)},
            device_id_type=MESH,
        )
        return c

    small = [
        pltpu.make_async_copy(src, dst, small_sem.at[i])
        for i, (src, dst) in enumerate((
            (rows_hbm, rows_ref), (partners_hbm, partners_ref), (counts_hbm, counts_ref),
            (start_hbm, start_ref), (contact_hbm, contact_ref), (load_hbm, load_ref),
        ))
    ]
    for copy in small:
        copy.start()
    chunks = width // CHUNK
    for c in range(chunks):
        pltpu.make_async_copy(
            block_hbm.at[0, 0, pl.ds(c * CHUNK, CHUNK)], block_f32.at[pl.ds(c * CHUNK, CHUNK)],
            block_sem.at[c],
        ).start()
    lax.fori_loop(1, total, greet, 0, unroll=True)

    k_of = lax.broadcasted_iota(jnp.int32, (jr, lanes), 0)
    l_of = lax.broadcasted_iota(jnp.int32, (jr, lanes), 1)
    spread = jnp.where(lax.rem(l_of, jr) == k_of, 1.0, 0.0).astype(BF16)
    for copy in small:
        copy.wait()
    rows_f = jnp.concatenate([rows_ref[r] for r in range(rounds)], axis=0).astype(F32)
    r_hi = rows_f.astype(BF16)
    r_lo = (rows_f - r_hi.astype(F32)).astype(BF16)
    tiled = jnp.dot(r_hi, spread, preferred_element_type=F32) + jnp.dot(
        r_lo, spread, preferred_element_type=F32
    )
    lane = lax.broadcasted_iota(jnp.int32, (1, lanes), 1)
    lane_q = lane // jr
    lane_k = lax.rem(lane, jr)
    slot = jnp.full((1, lanes), -1.0, F32)
    for r in range(rounds):
        mine = (lane_q == partners_ref[0, r]) & (lane_k < counts_ref[0, 0, r])
        slot = jnp.where(mine, tiled[r : r + 1], slot)
    for c in range(width // 128):
        ids = lax.broadcasted_iota(jnp.int32, (128, lanes), 0).astype(F32) + float(c * 128)
        select[pl.ds(c * 128, 128), :] = jnp.where(ids == slot, 1.0, 0.0).astype(BF16)

    def gather(x):
        return fold(jnp.dot(split3(x), select[...], preferred_element_type=F32), 3)

    def scatter(x):
        y = lax.dot_general(
            split3(x), select[...], (((1,), (1,)), ((), ())), preferred_element_type=F32
        )
        return fold(y, 3)

    def times(xs, hi, lo):
        y = jnp.dot(xs, hi, preferred_element_type=F32) + jnp.dot(
            xs, lo, preferred_element_type=F32
        )
        return fold(y, 2)

    def matvec(x):
        return times(split2(x), block_hi[...], block_lo[...])

    def pick(dst, src):
        def body(c, carry):
            part = pl.ds(pl.multiple_of(c * CHUNK, CHUNK), CHUNK)
            a = jnp.dot(src[part, :], select[...], preferred_element_type=F32)
            dst[part, :lanes] = a.astype(BF16)
            dst[part, lanes : lanes + FACE] = src[part, :FACE]
            dst[part, lanes + FACE :] = src[part, width - FACE :]
            return carry

        lax.fori_loop(0, chunks, body, 0)

    sub_id = lax.broadcasted_iota(jnp.int32, (loads, 128), 0)
    group_id = lax.broadcasted_iota(jnp.int32, (loads, 128), 1) // jr

    def swap(x):
        b = 1
        while b < per:
            sb = lax.rem(sub_id // b, 2)
            gb = lax.rem(group_id // b, 2)
            down = pltpu.roll(pltpu.roll(x, b, 0), 128 - b * jr, 1)
            up = pltpu.roll(pltpu.roll(x, loads - b, 0), b * jr, 1)
            x = jnp.where(sb == gb, x, jnp.where(sb == 1, down, up))
            b *= 2
        return x

    def put_rows(x, dst):
        for j in range(tiles):
            t = swap(x[:, j * 128 : (j + 1) * 128])
            for g in range(per):
                for a in range(halves):
                    dst[j * per + g, a] = t[a * per + g : a * per + g + 1]

    def get_rows(src):
        parts = []
        for j in range(tiles):
            t = [src[j * per + g, a] for a in range(halves) for g in range(per)]
            parts.append(swap(jnp.concatenate(t, axis=0)))
        return jnp.concatenate(parts, axis=1)

    def rows_copy(src, dst, send_sem, recv_sem):
        def copy(o):
            q = lax.rem(plan + side * o + plans, plans)
            return pltpu.make_async_remote_copy(
                src.at[q], dst.at[plan], send_sem, recv_sem,
                device_id={"plan": q, "layer": layer}, device_id_type=MESH,
            )

        return copy

    def start_all(copy, n):
        def body(o, c):
            copy(n - o).start()
            return c

        lax.fori_loop(1, n, body, 0, unroll=True)

    def drain(ref, n, sem):
        whole = ref.at[pl.ds(0, n)]
        pltpu.make_async_copy(whole, whole, sem).wait()

    def face_copies(src, dst, send_sem, recv_sem, first, last):
        up = pltpu.make_async_remote_copy(
            last(src), dst.at[0], send_sem.at[0], recv_sem.at[0],
            device_id={"plan": plan, "layer": lax.rem(layer + 1, layers)}, device_id_type=MESH,
        )
        down = pltpu.make_async_remote_copy(
            first(src), dst.at[1], send_sem.at[1], recv_sem.at[1],
            device_id={"plan": plan, "layer": lax.rem(layer + layers - 1, layers)}, device_id_type=MESH,
        )
        return up, down

    has_up = layer < layers - 1
    has_down = layer > 0

    def face_start(copies):
        up, down = copies

        @pl.when(has_up)
        def _():
            up.start()

        @pl.when(has_down)
        def _():
            down.start()

    def face_wait(copies):
        up, down = copies

        @pl.when(has_up)
        def _():
            up.wait_send()
            down.wait_recv()

        @pl.when(has_down)
        def _():
            down.wait_send()
            up.wait_recv()

    def get_flags(src):
        mine = lax.rem(plan, per)
        parts = []
        for j in range(tiles):
            acc = jnp.zeros((8, 128), F32)
            for g in range(per):
                shift = lax.rem(g + per - mine, per) * jr
                row = jnp.broadcast_to(src[j * per + g, halves], (8, 128))
                acc = jnp.where(group_id == g, pltpu.roll(row, shift, 1), acc)
            parts.append(acc)
        return jnp.concatenate(parts, axis=1)

    def meet_copy(end, there, w):
        low, high = (place, w) if end == 0 else (w, place)
        q = part_of + (high // 2) * 2 + lax.rem(low, 2)
        slot = (low // 2) * 2 + lax.rem(high, 2)
        return pltpu.make_async_remote_copy(
            send_rows.at[there * part_of + w], meet.at[0 if end == 0 else 1, slot],
            meet_send_sem.at[w], meet_sem.at[0 if end == 0 else 1],
            device_id={"plan": q, "layer": layer}, device_id_type=MESH,
        )

    start_m = start_ref[0, 0]
    load = load_ref[0, 0]
    con = jnp.where(contact_ref[0] == 1, 1.0, 0.0)
    mr0 = gather(start_m)
    oc0 = jnp.dot(
        jnp.broadcast_to(con, (16, width)).astype(BF16), select[...], preferred_element_type=F32
    )[:8]
    m_rows[...] = mr0
    own_con[...] = oc0
    out_m[0, 0] = start_m
    put_rows(mr0, init_send)
    for q in range(plans):
        j = q // per
        init_send[q, halves] = oc0[:1, j * 128 : (j + 1) * 128]
    fcon_send[0] = jnp.broadcast_to(con[:, :FACE], (8, FACE))
    fcon_send[1] = jnp.broadcast_to(con[:, width - FACE :], (8, FACE))
    init_rows[plan] = jnp.zeros((halves + 1, 1, 128), F32)
    for s in range(2):
        recv_rows[s, plan] = jnp.zeros((halves, 1, 128), F32)

    @pl.when(layer == 0)
    def _():
        init_face[0] = jnp.zeros((loads, FACE), F32)
        recv_face[0] = jnp.zeros((loads, FACE), F32)
        fcon_recv[0] = jnp.zeros((8, FACE), F32)

    @pl.when(layer == layers - 1)
    def _():
        init_face[1] = jnp.zeros((loads, FACE), F32)
        recv_face[1] = jnp.zeros((loads, FACE), F32)
        fcon_recv[1] = jnp.zeros((8, FACE), F32)

    for s in range(2):
        ar_recv[s, me] = jnp.zeros((1, 128), F32)

    pl.semaphore_wait(barrier, total - 1)

    m_faces = face_copies(
        start_ref, init_face, init_face_send_sem, init_face_sem,
        lambda r: r.at[0, 0, :, pl.ds(0, FACE)], lambda r: r.at[0, 0, :, pl.ds(width - FACE, FACE)],
    )
    c_faces = face_copies(
        fcon_send, fcon_recv, fcon_send_sem, fcon_recv_sem, lambda r: r.at[0], lambda r: r.at[1]
    )
    g_faces = face_copies(
        face_send, recv_face, face_send_sem, face_recv_sem, lambda r: r.at[0], lambda r: r.at[1]
    )
    start_all(rows_copy(init_send, init_rows, init_send_sem, init_rows_sem), plans)
    face_start(m_faces)
    face_start(c_faces)

    xs = split2(start_m)
    y = None
    for c in range(chunks):
        part = pl.ds(c * CHUNK, CHUNK)
        pltpu.make_async_copy(block_hbm.at[0, 0, part], block_f32.at[part], block_sem.at[c]).wait()
        a = block_f32[part, :]
        hi = a.astype(BF16)
        lo = (a - hi.astype(F32)).astype(BF16)
        block_hi[part, :] = hi
        block_lo[part, :] = lo
        xc = xs[:, c * CHUNK : (c + 1) * CHUNK]
        t = jnp.dot(xc, hi, preferred_element_type=F32) + jnp.dot(xc, lo, preferred_element_type=F32)
        y = t if y is None else y + t
    base = fold(y, 2) - load
    base_r = gather(base)
    put_rows(base_r, send_rows)
    face_send[0] = base[:, :FACE]
    face_send[1] = base[:, width - FACE :]
    start_all(rows_copy(send_rows, recv_rows.at[0], rows_send_sem, rows_recv_sem.at[0, 0]), plans)
    face_start(g_faces)

    pick(front_hi, block_hi)
    drain(init_rows, plans - 1, init_rows_sem)
    face_wait(m_faces)
    face_wait(c_faces)
    h_con[...] = get_flags(init_rows)

    sub = lax.broadcasted_iota(jnp.int32, (loads, 128), 0)
    ln = lax.broadcasted_iota(jnp.int32, (loads, 128), 1)
    contact_all = jnp.broadcast_to(con, (loads, width)) > 0.5

    def folded(x):
        t = x[:, :128]
        for j in range(1, x.shape[1] // 128):
            t = t + x[:, j * 128 : (j + 1) * 128]
        return t

    def local_sums(g, gr):
        ga = matvec(g)
        gs = jnp.sum(g * g, axis=1, keepdims=True)
        g_lo = g[:, :FACE]
        g_hi = g[:, width - FACE :]
        curved = folded(g * ga) + folded(gr * gr) + (g_lo * g_lo + g_hi * g_hi)
        return jnp.where(ln == sub, gs, 0.0), curved

    def sums_start(s, squares, curved):
        cv = jnp.sum(curved, axis=1, keepdims=True)
        mine = jnp.where(ln == sub + loads, cv, squares)
        mine = jnp.sum(mine, axis=0, keepdims=True)
        ar_send[0] = mine

        def ar_copy(o):
            d = lax.rem(me + side * o + total, total)
            return pltpu.make_async_remote_copy(
                ar_send.at[0], ar_recv.at[s, me], ar_send_sem, ar_recv_sem.at[s],
                device_id={"plan": d // layers, "layer": lax.rem(d, layers)}, device_id_type=MESH,
            )

        start_all(ar_copy, total)
        return mine

    def sums_end(s, mine):
        drain(ar_recv.at[s], total - 1, ar_recv_sem.at[s])
        sums = mine + jnp.sum(ar_recv[s], axis=0)
        sums = jnp.broadcast_to(sums, (loads, 128))
        num = jnp.sum(jnp.where(ln == sub, sums, 0.0), axis=1, keepdims=True)
        den = jnp.sum(jnp.where(ln == sub + loads, sums, 0.0), axis=1, keepdims=True)
        drain(ar_recv.at[s], total - 1, ar_send_sem)
        return (num + 1e-6) / (den + 1e-6)

    def move_all(alpha, m, g, mr, gr, hm, hg, below, above):
        def move(x, grad, flag):
            moved = x - alpha * grad
            return jnp.where(flag, jnp.maximum(moved, 0.0), moved)

        out_m[0, 0] = move(m, g, contact_all)
        m_rows[...] = move(mr, gr, own_con[...] > 0.5)
        h_rows[...] = move(hm, hg, h_con[...] > 0.5)
        h_face[0] = move(h_face[0], below, fcon_recv[0] > 0.5)
        h_face[1] = move(h_face[1], above, fcon_recv[1] > 0.5)

    hm0 = get_rows(init_rows)
    apart = mr0 - hm0
    low_apart = start_m[:, :FACE] - init_face[0]
    high_apart = start_m[:, width - FACE :] - init_face[1]
    h_face[0] = init_face[0]
    h_face[1] = init_face[1]
    gr0 = base_r + apart
    g0 = base + scatter(apart)
    g0 = jnp.concatenate(
        [g0[:, :FACE] + low_apart, g0[:, FACE : width - FACE], g0[:, width - FACE :] + high_apart], axis=1
    )
    out_g[0, 0] = g0
    squares0, curved0 = local_sums(g0, gr0)
    face_wait(g_faces)
    below0 = jnp.where(has_down, recv_face[0] - low_apart, 0.0)
    above0 = jnp.where(has_up, recv_face[1] - high_apart, 0.0)
    curved0 = curved0 - (g0[:, :FACE] * below0 + g0[:, width - FACE :] * above0)
    drain(recv_rows.at[0], plans - 1, rows_recv_sem.at[0, 0])
    hg0 = get_rows(recv_rows.at[0]) - apart
    mine0 = sums_start(0, squares0, curved0 - folded(gr0 * hg0))
    pick(front_lo, block_lo)
    load_rows[...] = gather(load)
    drain(recv_rows.at[0], plans - 1, rows_send_sem)
    drain(init_rows, plans - 1, init_send_sem)
    alpha0 = sums_end(0, mine0)
    move_all(alpha0, start_m, g0, mr0, gr0, hm0, hg0, below0, above0)

    def step(it, carry):
        m = out_m[0, 0]
        mr = m_rows[...]
        hm = h_rows[...]
        load = load_ref[0, 0]
        s = lax.rem(it, 2)
        apart = mr - hm
        xs = split2(m)
        gr = times(xs, front_hi[:, :lanes], front_lo[:, :lanes]) + (apart - load_rows[...])
        put_rows(gr, send_rows)
        ends = times(xs, front_hi[:, lanes:], front_lo[:, lanes:])
        g_lo = ends[:, :FACE] + (m[:, :FACE] - h_face[0]) - load[:, :FACE]
        g_hi = ends[:, FACE:] + (m[:, width - FACE :] - h_face[1]) - load[:, width - FACE :]
        face_send[0] = g_lo
        face_send[1] = g_hi
        for end, there in ((0, PLANES - 1), (PLANES - 1, 0)):

            @pl.when(plane == end)
            def _(end=end, there=there):
                for w in range(part_of):
                    meet_copy(end, there, w).start()

        start_all(rows_copy(send_rows, recv_rows.at[s], rows_send_sem, rows_recv_sem.at[s, plane]), plans)
        face_start(g_faces)
        inner = pl.ds(FACE, width - 2 * FACE)
        mid = times(xs, block_hi[:, inner], block_lo[:, inner])
        mid = mid + scatter(apart)[:, FACE : width - FACE] - load[:, FACE : width - FACE]
        g = jnp.concatenate([g_lo, mid, g_hi], axis=1)
        out_g[0, 0] = g
        squares, curved = local_sums(g, gr)
        face_wait(g_faces)
        below = recv_face[0]
        above = recv_face[1]
        curved = curved - (g_lo * below + g_hi * above)
        came = recv_rows.at[s]
        drain(came, part_of - 1, rows_recv_sem.at[s, plane])

        @pl.when(plane % (PLANES - 1) == 0)
        def _():
            acc = jnp.zeros((halves, 1, 128), F32)
            for w in range(part_of):
                q = plane * part_of + w
                acc = acc + send_rows[q] * came[q]
            products[...] = acc

        @pl.when(plane % (PLANES - 1) != 0)
        def _():
            for step_by in range(1, PLANES):
                drain(came, part_of, rows_recv_sem.at[s, lax.rem(plane + step_by, PLANES)])
            acc = jnp.zeros((halves, 1, 128), F32)
            for q in range(plans):
                weight = 2.0 if (q // part_of) % (PLANES - 1) == 0 else 1.0
                acc = acc + weight * (send_rows[q] * came[q])
            products[...] = acc

        @pl.when(plane == 1)
        def _():
            drain(meet.at[0], part_of, meet_sem.at[0])
            drain(meet.at[1], part_of, meet_sem.at[1])
            acc = products[...]
            for w in range(part_of):
                acc = acc + 2.0 * (meet[0, w] * meet[1, w])
            products[...] = acc

        shared = jnp.zeros((loads, 128), F32)
        for a in range(halves):
            row = jnp.broadcast_to(products[a], (loads, 128))
            shared = jnp.where(sub_id // per == a, row, shared)
        curved = curved - jnp.where(group_id == lax.rem(sub_id, per), shared, 0.0)
        mine = sums_start(s, squares, curved)

        @pl.when(plane % (PLANES - 1) == 0)
        def _():
            for step_by in range(1, PLANES):
                drain(came, part_of, rows_recv_sem.at[s, lax.rem(plane + step_by, PLANES)])

            for w in range(part_of):
                meet_copy(0, PLANES - 1, w).wait_send()

        drain(came, plans - 1, rows_send_sem)
        hg = get_rows(came)
        alpha = sums_end(s, mine)
        move_all(alpha, m, g, mr, gr, hm, hg, below, above)
        return carry

    lax.fori_loop(1, ITERS, step, 0)


def shards(plans, layers, dual_block, start, load, partners, jump_rows, counts, contact):
    loads, width = start.shape[2], start.shape[3]
    jr = jump_rows.shape[3]
    lanes = plans * jr
    halves = loads * jr // 128
    jump_rows = jump_rows.reshape(jump_rows.shape[2], 1, jr)
    total = plans * layers
    vmem = pl.BlockSpec(memory_space=pltpu.VMEM)
    dma = pltpu.SemaphoreType.DMA
    out = jax.ShapeDtypeStruct((2, 1, loads, width), F32)
    both = pl.pallas_call(
        functools.partial(kernel, plans, layers),
        out_shape=out,
        in_specs=[pl.BlockSpec(memory_space=pl.ANY)] * 7,
        out_specs=vmem,
        scratch_shapes=[
            pltpu.VMEM(start.shape, F32),
            pltpu.VMEM(load.shape, F32),
            pltpu.SMEM(partners.shape, jnp.int32),
            pltpu.VMEM(jump_rows.shape, jnp.int32),
            pltpu.SMEM(counts.shape, jnp.int32),
            pltpu.VMEM(contact.shape, jnp.int32),
            pltpu.VMEM((width, width), F32),
            pltpu.VMEM((width, width), BF16),
            pltpu.VMEM((width, width), BF16),
            pltpu.VMEM((width, lanes), BF16),
            pltpu.VMEM((width, lanes + 2 * FACE), BF16),
            pltpu.VMEM((width, lanes + 2 * FACE), BF16),
            pltpu.VMEM((plans, halves + 1, 1, 128), F32),
            pltpu.VMEM((plans, halves, 1, 128), F32),
            pltpu.VMEM((plans, halves + 1, 1, 128), F32),
            pltpu.VMEM((2, plans, halves, 1, 128), F32),
            pltpu.VMEM((2, loads, FACE), F32),
            pltpu.VMEM((2, loads, FACE), F32),
            pltpu.VMEM((2, plans // PLANES, halves, 1, 128), F32),
            pltpu.VMEM((2, 8, FACE), F32),
            pltpu.VMEM((2, 8, FACE), F32),
            pltpu.VMEM((1, 1, 128), F32),
            pltpu.VMEM((2, total, 1, 128), F32),
            pltpu.VMEM((halves, 1, 128), F32),
            pltpu.VMEM((loads, lanes), F32),
            pltpu.VMEM((loads, lanes), F32),
            pltpu.VMEM((8, lanes), F32),
            pltpu.VMEM((8, lanes), F32),
            pltpu.VMEM((2, loads, FACE), F32),
            pltpu.VMEM((loads, lanes), F32),
            pltpu.VMEM((2, loads, FACE), F32),
            dma((6,)), dma((width // CHUNK,)),
            dma, dma, dma((2, PLANES)), dma((2,)), dma((plans // PLANES,)), dma((2,)),
            dma((2,)), dma((2,)), dma((2,)), dma((2,)),
            dma, dma((2,)),
            dma, dma((2,)),
        ],
        compiler_params=pltpu.CompilerParams(
            collective_id=0, has_side_effects=True, vmem_limit_bytes=67_000_000
        ),
        name="dual_steps",
    )(dual_block, start, load, partners, jump_rows, counts, contact)
    return both[:1], both[1:]


def solution(mesh):
    block = P("layer", "plan", None, None)
    in_specs = (
        block, block, block, P("plan", None), block, P("layer", "plan", None), P("layer", "plan", None),
    )
    body = functools.partial(shards, mesh.shape["plan"], mesh.shape["layer"])
    return jax.shard_map(
        body, mesh=mesh, in_specs=in_specs, out_specs=(block, block), check_vma=False
    )
```

```python
import functools

import jax
import jax.numpy as jnp
from jax import lax
from jax.experimental import pallas as pl
from jax.experimental.pallas import tpu as pltpu
from jax.sharding import PartitionSpec as P

FACE = 128
ITERS = 4
PLANES = 4
CHUNK = 256
MESH = pl.DeviceIdType.MESH
F32 = jnp.float32
BF16 = jnp.bfloat16


def split2(x):
    hi = x.astype(BF16)
    lo = (x - hi.astype(F32)).astype(BF16)
    return jnp.concatenate([hi, lo], axis=0)


def split3(x):
    hi = x.astype(BF16)
    rest = x - hi.astype(F32)
    mid = rest.astype(BF16)
    lo = (rest - mid.astype(F32)).astype(BF16)
    return jnp.concatenate([hi, mid, lo], axis=0)


def fold(y, parts):
    n = y.shape[0] // parts
    total = y[:n]
    for i in range(1, parts):
        total = total + y[i * n : (i + 1) * n]
    return total


def kernel(
    plans, layers, block_hbm, start_hbm, load_hbm, partners_hbm, rows_hbm, counts_hbm, contact_hbm,
    out_ref,
    start_ref, load_ref, partners_ref, rows_ref, counts_ref, contact_ref,
    block_f32, block_hi, block_lo, select, front_hi, front_lo,
    init_send, send_rows, init_rows, recv_rows, init_face, recv_face, meet, fcon_send, fcon_recv, ar_send, ar_recv,
    products, m_rows, h_rows, h_con, own_con, h_face, load_rows, face_send, pack_g, pack_d,
    small_sem, block_sem, rows_send_sem, init_rows_sem, rows_recv_sem, init_face_sem, meet_send_sem, meet_sem,
    face_send_sem, face_recv_sem, fcon_send_sem, fcon_recv_sem, ar_send_sem, ar_recv_sem,
    init_send_sem, init_face_send_sem,
):
    out_m, out_g = out_ref.at[pl.ds(0, 1)], out_ref.at[pl.ds(1, 1)]
    rounds, jr = rows_ref.shape[0], rows_ref.shape[2]
    loads, width = start_ref.shape[2], start_ref.shape[3]
    lanes = plans * jr
    per = 128 // jr
    halves = loads // per
    tiles = lanes // 128
    total = plans * layers
    part_of = plans // PLANES
    plan = lax.axis_index("plan")
    layer = lax.axis_index("layer")
    me = plan * layers + layer

    plane = plan // part_of
    place = lax.rem(plan, part_of)
    near = part_of * layers
    spot = me - plane * near
    far = (PLANES - 1) * (1 - (2 * plane) // PLANES)
    second = lax.rem(2 + (PLANES - 1) * plane, PLANES + 1)
    third = 1 + lax.rem(plane, 2)
    at_end = plane % (PLANES - 1) == 0
    barrier = pltpu.get_barrier_semaphore()

    def greet(o, c):
        d = lax.rem(me + o, total)
        pl.semaphore_signal(
            barrier, inc=1, device_id={"plan": d // layers, "layer": lax.rem(d, layers)},
            device_id_type=MESH,
        )
        return c

    small = [
        pltpu.make_async_copy(src, dst, small_sem.at[i])
        for i, (src, dst) in enumerate((
            (rows_hbm, rows_ref), (partners_hbm, partners_ref), (counts_hbm, counts_ref),
            (start_hbm, start_ref), (contact_hbm, contact_ref), (load_hbm, load_ref),
        ))
    ]
    for copy in small:
        copy.start()
    chunks = width // CHUNK
    for c in range(chunks):
        pltpu.make_async_copy(
            block_hbm.at[0, 0, pl.ds(c * CHUNK, CHUNK)], block_f32.at[pl.ds(c * CHUNK, CHUNK)],
            block_sem.at[c],
        ).start()
    lax.fori_loop(1, total, greet, 0, unroll=True)

    k_of = lax.broadcasted_iota(jnp.int32, (jr, lanes), 0)
    l_of = lax.broadcasted_iota(jnp.int32, (jr, lanes), 1)
    spread = jnp.where(lax.rem(l_of, jr) == k_of, 1.0, 0.0).astype(BF16)
    for copy in small:
        copy.wait()
    rows_f = jnp.concatenate([rows_ref[r] for r in range(rounds)], axis=0).astype(F32)
    r_hi = rows_f.astype(BF16)
    r_lo = (rows_f - r_hi.astype(F32)).astype(BF16)
    tiled = jnp.dot(r_hi, spread, preferred_element_type=F32) + jnp.dot(
        r_lo, spread, preferred_element_type=F32
    )
    lane = lax.broadcasted_iota(jnp.int32, (1, lanes), 1)
    lane_q = lane // jr
    lane_k = lax.rem(lane, jr)
    slot = jnp.full((1, lanes), -1.0, F32)
    for r in range(rounds):
        mine = (lane_q == partners_ref[0, r]) & (lane_k < counts_ref[0, 0, r])
        slot = jnp.where(mine, tiled[r : r + 1], slot)
    for c in range(width // 128):
        ids = lax.broadcasted_iota(jnp.int32, (128, lanes), 0).astype(F32) + float(c * 128)
        select[pl.ds(c * 128, 128), :] = jnp.where(ids == slot, 1.0, 0.0).astype(BF16)

    def gather(x):
        return fold(jnp.dot(split3(x), select[...], preferred_element_type=F32), 3)

    def scatter(x):
        y = lax.dot_general(
            split3(x), select[...], (((1,), (1,)), ((), ())), preferred_element_type=F32
        )
        return fold(y, 3)

    def times(xs, hi, lo):
        y = jnp.dot(xs, hi, preferred_element_type=F32) + jnp.dot(
            xs, lo, preferred_element_type=F32
        )
        return fold(y, 2)

    def matvec(x):
        return times(split2(x), block_hi[...], block_lo[...])

    def pick(dst, src):
        def body(c, carry):
            part = pl.ds(pl.multiple_of(c * CHUNK, CHUNK), CHUNK)
            a = jnp.dot(src[part, :], select[...], preferred_element_type=F32)
            dst[part, :lanes] = a.astype(BF16)
            dst[part, lanes : lanes + FACE] = src[part, :FACE]
            dst[part, lanes + FACE :] = src[part, width - FACE :]
            return carry

        lax.fori_loop(0, chunks, body, 0)

    sub_id = lax.broadcasted_iota(jnp.int32, (loads, 128), 0)
    group_id = lax.broadcasted_iota(jnp.int32, (loads, 128), 1) // jr

    def swap(x):
        b = 1
        while b < per:
            sb = lax.rem(sub_id // b, 2)
            gb = lax.rem(group_id // b, 2)
            down = pltpu.roll(pltpu.roll(x, b, 0), 128 - b * jr, 1)
            up = pltpu.roll(pltpu.roll(x, loads - b, 0), b * jr, 1)
            x = jnp.where(sb == gb, x, jnp.where(sb == 1, down, up))
            b *= 2
        return x

    def put_rows(x, dst):
        for j in range(tiles):
            t = swap(x[:, j * 128 : (j + 1) * 128])
            for g in range(per):
                for a in range(halves):
                    dst[j * per + g, a] = t[a * per + g : a * per + g + 1]

    def get_rows(src):
        parts = []
        for j in range(tiles):
            t = [src[j * per + g, a] for a in range(halves) for g in range(per)]
            parts.append(swap(jnp.concatenate(t, axis=0)))
        return jnp.concatenate(parts, axis=1)

    def rows_copy(src, dst, send_sem, recv_sem):
        def copy(z, o):
            q = z * part_of + lax.rem(place + o, part_of)
            return pltpu.make_async_remote_copy(
                src.at[q], dst.at[plan], send_sem, recv_sem,
                device_id={"plan": q, "layer": layer}, device_id_type=MESH,
            )

        return copy

    def start_plane(copy, z, first, n):
        def body(o, c):
            copy(z, o).start()
            return c

        lax.fori_loop(first, n, body, 0, unroll=True)

    def start_rows(copy):
        for z in (far, second, third):
            start_plane(copy, z, 0, part_of)
        start_plane(copy, plane, 1, part_of)

    def drain(ref, n, sem):
        whole = ref.at[pl.ds(0, n)]
        pltpu.make_async_copy(whole, whole, sem).wait()

    def face_copies(src, dst, send_sem, recv_sem, first, last):
        up = pltpu.make_async_remote_copy(
            last(src), dst.at[0], send_sem.at[0], recv_sem.at[0],
            device_id={"plan": plan, "layer": lax.rem(layer + 1, layers)}, device_id_type=MESH,
        )
        down = pltpu.make_async_remote_copy(
            first(src), dst.at[1], send_sem.at[1], recv_sem.at[1],
            device_id={"plan": plan, "layer": lax.rem(layer + layers - 1, layers)}, device_id_type=MESH,
        )
        return up, down

    has_up = layer < layers - 1
    has_down = layer > 0

    def face_start(copies):
        up, down = copies

        @pl.when(has_up)
        def _():
            up.start()

        @pl.when(has_down)
        def _():
            down.start()

    def face_wait(copies):
        up, down = copies

        @pl.when(has_up)
        def _():
            up.wait_send()
            down.wait_recv()

        @pl.when(has_down)
        def _():
            down.wait_send()
            up.wait_recv()

    def get_flags(src):
        mine = lax.rem(plan, per)
        parts = []
        for j in range(tiles):
            acc = jnp.zeros((8, 128), F32)
            for g in range(per):
                shift = lax.rem(g + per - mine, per) * jr
                row = jnp.broadcast_to(src[j * per + g, halves], (8, 128))
                acc = jnp.where(group_id == g, pltpu.roll(row, shift, 1), acc)
            parts.append(acc)
        return jnp.concatenate(parts, axis=1)

    def meet_copy(s, end, there, w):
        low, high = (place, w) if end == 0 else (w, place)
        q = part_of + (high // 2) * 2 + lax.rem(low, 2)
        slot = (low // 2) * 2 + lax.rem(high, 2)
        return pltpu.make_async_remote_copy(
            send_rows.at[there * part_of + w], meet.at[s, 0 if end == 0 else 1, slot],
            meet_send_sem.at[w], meet_sem.at[s, 0 if end == 0 else 1],
            device_id={"plan": q, "layer": layer}, device_id_type=MESH,
        )

    start_m = start_ref[0, 0]
    load = load_ref[0, 0]
    con = jnp.where(contact_ref[0] == 1, 1.0, 0.0)
    mr0 = gather(start_m)
    oc0 = jnp.dot(
        jnp.broadcast_to(con, (16, width)).astype(BF16), select[...], preferred_element_type=F32
    )[:8]
    m_rows[...] = mr0
    own_con[...] = oc0
    out_m[0, 0] = start_m
    put_rows(mr0, init_send)
    for q in range(plans):
        j = q // per
        init_send[q, halves] = oc0[:1, j * 128 : (j + 1) * 128]
    fcon_send[0] = jnp.broadcast_to(con[:, :FACE], (8, FACE))
    fcon_send[1] = jnp.broadcast_to(con[:, width - FACE :], (8, FACE))
    init_rows[plan] = jnp.zeros((halves + 1, 1, 128), F32)
    for s in range(2):
        recv_rows[s, plan] = jnp.zeros((halves, 1, 128), F32)

    @pl.when(layer == 0)
    def _():
        init_face[0] = jnp.zeros((loads, FACE), F32)
        recv_face[0] = jnp.zeros((loads, FACE), F32)
        fcon_recv[0] = jnp.zeros((8, FACE), F32)

    @pl.when(layer == layers - 1)
    def _():
        init_face[1] = jnp.zeros((loads, FACE), F32)
        recv_face[1] = jnp.zeros((loads, FACE), F32)
        fcon_recv[1] = jnp.zeros((8, FACE), F32)

    for s in range(2):
        ar_recv[s, me] = jnp.zeros((1, 128), F32)

    pl.semaphore_wait(barrier, total - 1)

    m_faces = face_copies(
        start_ref, init_face, init_face_send_sem, init_face_sem,
        lambda r: r.at[0, 0, :, pl.ds(0, FACE)], lambda r: r.at[0, 0, :, pl.ds(width - FACE, FACE)],
    )
    c_faces = face_copies(
        fcon_send, fcon_recv, fcon_send_sem, fcon_recv_sem, lambda r: r.at[0], lambda r: r.at[1]
    )
    g_faces = face_copies(
        face_send, recv_face, face_send_sem, face_recv_sem, lambda r: r.at[0], lambda r: r.at[1]
    )
    start_rows(rows_copy(init_send, init_rows, init_send_sem, init_rows_sem))
    face_start(m_faces)
    face_start(c_faces)

    xs = split2(start_m)
    y = None
    for c in range(chunks):
        part = pl.ds(c * CHUNK, CHUNK)
        pltpu.make_async_copy(block_hbm.at[0, 0, part], block_f32.at[part], block_sem.at[c]).wait()
        a = block_f32[part, :]
        hi = a.astype(BF16)
        lo = (a - hi.astype(F32)).astype(BF16)
        block_hi[part, :] = hi
        block_lo[part, :] = lo
        xc = xs[:, c * CHUNK : (c + 1) * CHUNK]
        t = jnp.dot(xc, hi, preferred_element_type=F32) + jnp.dot(xc, lo, preferred_element_type=F32)
        y = t if y is None else y + t
    base = fold(y, 2) - load
    base_r = gather(base)
    put_rows(base_r, send_rows)
    face_send[0] = base[:, :FACE]
    face_send[1] = base[:, width - FACE :]
    start_rows(rows_copy(send_rows, recv_rows.at[0], rows_send_sem, rows_recv_sem.at[0, plane]))
    face_start(g_faces)

    pick(front_hi, block_hi)
    drain(init_rows, plans - 1, init_rows_sem)
    face_wait(m_faces)
    face_wait(c_faces)
    h_con[...] = get_flags(init_rows)

    sub = lax.broadcasted_iota(jnp.int32, (loads, 128), 0)
    ln = lax.broadcasted_iota(jnp.int32, (loads, 128), 1)
    contact_all = jnp.broadcast_to(con, (loads, width)) > 0.5

    def folded(x):
        t = x[:, :128]
        for j in range(1, x.shape[1] // 128):
            t = t + x[:, j * 128 : (j + 1) * 128]
        return t

    def local_sums(g, gr):
        ga = matvec(g)
        gs = jnp.sum(g * g, axis=1, keepdims=True)
        g_lo = g[:, :FACE]
        g_hi = g[:, width - FACE :]
        curved = folded(g * ga) + folded(gr * gr) + (g_lo * g_lo + g_hi * g_hi)
        return jnp.where(ln == sub, gs, 0.0), curved

    def sums_start(s, squares, curved, left, right, meets):
        def products_of(z):
            acc = jnp.zeros((halves, 1, 128), F32)
            for w in range(part_of):
                q = z * part_of + w
                acc = acc + left[q] * right(q)
            return acc

        def arrive(z, n):
            drain(recv_rows.at[s], n, rows_recv_sem.at[s, z])

        def message(slot, shared_rows):
            shared = jnp.zeros((loads, 128), F32)
            for a in range(halves):
                row = jnp.broadcast_to(shared_rows[a], (loads, 128))
                shared = jnp.where(sub_id // per == a, row, shared)
            shared = jnp.where(group_id == lax.rem(sub_id, per), shared, 0.0)
            cv = jnp.sum(curved - shared, axis=1, keepdims=True)
            mine = jnp.where(ln == sub + loads, cv, squares)
            ar_send[slot] = jnp.sum(mine, axis=0, keepdims=True)

        def send(slot, z, first=0):
            def copy(z, o):
                d = z * near + lax.rem(spot + o, near)
                return pltpu.make_async_remote_copy(
                    ar_send.at[slot], ar_recv.at[s, me], ar_send_sem, ar_recv_sem.at[s],
                    device_id={"plan": d // layers, "layer": lax.rem(d, layers)}, device_id_type=MESH,
                )

            start_plane(copy, z, first, near)

        arrive(plane, part_of - 1)
        own = products_of(plane)

        @pl.when(at_end)
        def _():
            message(1, own)
            send(1, far)
            send(1, second)
            if meets:
                send(1, third)
            arrive(third, part_of)
            arrive(second, part_of)
            some = own + 2.0 * (products_of(third) + products_of(second))
            arrive(far, part_of)
            last = 2.0 * products_of(far)
            message(0, some + last)
            if not meets:
                message(2, own + last)
            send(0, plane, 1)
            if not meets:
                send(2, third)

        @pl.when(jnp.logical_not(at_end))
        def _():
            arrive(second, part_of)
            one = own + 2.0 * products_of(second)
            message(1, one)
            send(1, far)
            arrive(third, part_of)
            other = 2.0 * products_of(third)
            arrive(far, part_of)
            last = 2.0 * products_of(far)
            products[...] = jnp.zeros((halves, 1, 128), F32)
            if meets:

                @pl.when(plane == 1)
                def _():
                    drain(meet.at[s, 0], part_of, meet_sem.at[s, 0])
                    drain(meet.at[s, 1], part_of, meet_sem.at[s, 1])
                    acc = jnp.zeros((halves, 1, 128), F32)
                    for w in range(part_of):
                        acc = acc + meet[s, 0, w] * meet[s, 1, w]
                    products[...] = 2.0 * acc

            met = products[...]
            message(2, one + last + met)
            message(3, own + other + last)
            message(0, one + other + last + met)
            send(2, third)
            send(3, second)
            send(0, plane, 1)

    def sums_end(s):
        drain(ar_recv.at[s], total - 1, ar_recv_sem.at[s])
        sums = ar_send[0] + jnp.sum(ar_recv[s], axis=0)
        sums = jnp.broadcast_to(sums, (loads, 128))
        num = jnp.sum(jnp.where(ln == sub, sums, 0.0), axis=1, keepdims=True)
        den = jnp.sum(jnp.where(ln == sub + loads, sums, 0.0), axis=1, keepdims=True)
        drain(ar_recv.at[s], total - 1, ar_send_sem)
        return (num + 1e-6) / (den + 1e-6)

    def move_all(alpha, m, g, mr, gr, hm, hg, below, above):
        def move(x, grad, flag):
            moved = x - alpha * grad
            return jnp.where(flag, jnp.maximum(moved, 0.0), moved)

        out_m[0, 0] = move(m, g, contact_all)
        m_rows[...] = move(mr, gr, own_con[...] > 0.5)
        h_rows[...] = move(hm, hg, h_con[...] > 0.5)
        h_face[0] = move(h_face[0], below, fcon_recv[0] > 0.5)
        h_face[1] = move(h_face[1], above, fcon_recv[1] > 0.5)

    hm0 = get_rows(init_rows)
    apart = mr0 - hm0
    low_apart = start_m[:, :FACE] - init_face[0]
    high_apart = start_m[:, width - FACE :] - init_face[1]
    h_face[0] = init_face[0]
    h_face[1] = init_face[1]
    gr0 = base_r + apart
    g0 = base + scatter(apart)
    g0 = jnp.concatenate(
        [g0[:, :FACE] + low_apart, g0[:, FACE : width - FACE], g0[:, width - FACE :] + high_apart], axis=1
    )
    out_g[0, 0] = g0
    put_rows(gr0, pack_g)
    put_rows(apart, pack_d)
    squares0, curved0 = local_sums(g0, gr0)
    face_wait(g_faces)
    below0 = jnp.where(has_down, recv_face[0] - low_apart, 0.0)
    above0 = jnp.where(has_up, recv_face[1] - high_apart, 0.0)
    curved0 = curved0 - (g0[:, :FACE] * below0 + g0[:, width - FACE :] * above0)
    sums_start(0, squares0, curved0, pack_g, lambda q: recv_rows[0, q] - pack_d[q], False)
    hg0 = get_rows(recv_rows.at[0]) - apart
    pick(front_lo, block_lo)
    load_rows[...] = gather(load)
    drain(recv_rows.at[0], plans - 1, rows_send_sem)
    drain(init_rows, plans - 1, init_send_sem)
    alpha0 = sums_end(0)
    move_all(alpha0, start_m, g0, mr0, gr0, hm0, hg0, below0, above0)

    def step(it, carry):
        m = out_m[0, 0]
        mr = m_rows[...]
        hm = h_rows[...]
        load = load_ref[0, 0]
        s = lax.rem(it, 2)
        apart = mr - hm
        xs = split2(m)
        gr = times(xs, front_hi[:, :lanes], front_lo[:, :lanes]) + (apart - load_rows[...])
        put_rows(gr, send_rows)
        ends = times(xs, front_hi[:, lanes:], front_lo[:, lanes:])
        g_lo = ends[:, :FACE] + (m[:, :FACE] - h_face[0]) - load[:, :FACE]
        g_hi = ends[:, FACE:] + (m[:, width - FACE :] - h_face[1]) - load[:, width - FACE :]
        face_send[0] = g_lo
        face_send[1] = g_hi
        for end, there in ((0, PLANES - 1), (PLANES - 1, 0)):

            @pl.when(plane == end)
            def _(end=end, there=there):
                for w in range(part_of):
                    meet_copy(s, end, there, w).start()

        start_rows(rows_copy(send_rows, recv_rows.at[s], rows_send_sem, rows_recv_sem.at[s, plane]))
        face_start(g_faces)
        inner = pl.ds(FACE, width - 2 * FACE)
        mid = times(xs, block_hi[:, inner], block_lo[:, inner])
        mid = mid + scatter(apart)[:, FACE : width - FACE] - load[:, FACE : width - FACE]
        g = jnp.concatenate([g_lo, mid, g_hi], axis=1)
        out_g[0, 0] = g
        squares, curved = local_sums(g, gr)
        face_wait(g_faces)
        below = recv_face[0]
        above = recv_face[1]
        curved = curved - (g_lo * below + g_hi * above)
        came = recv_rows.at[s]
        sums_start(s, squares, curved, send_rows, lambda q: came[q], True)

        @pl.when(at_end)
        def _():
            for w in range(part_of):
                meet_copy(s, 0, PLANES - 1, w).wait_send()

        drain(came, plans - 1, rows_send_sem)
        hg = get_rows(came)
        alpha = sums_end(s)
        move_all(alpha, m, g, mr, gr, hm, hg, below, above)
        return carry

    lax.fori_loop(1, ITERS, step, 0)


def shards(plans, layers, dual_block, start, load, partners, jump_rows, counts, contact):
    loads, width = start.shape[2], start.shape[3]
    jr = jump_rows.shape[3]
    lanes = plans * jr
    halves = loads * jr // 128
    jump_rows = jump_rows.reshape(jump_rows.shape[2], 1, jr)
    total = plans * layers
    vmem = pl.BlockSpec(memory_space=pltpu.VMEM)
    dma = pltpu.SemaphoreType.DMA
    out = jax.ShapeDtypeStruct((2, 1, loads, width), F32)
    both = pl.pallas_call(
        functools.partial(kernel, plans, layers),
        out_shape=out,
        in_specs=[pl.BlockSpec(memory_space=pl.ANY)] * 7,
        out_specs=vmem,
        scratch_shapes=[
            pltpu.VMEM(start.shape, F32),
            pltpu.VMEM(load.shape, F32),
            pltpu.SMEM(partners.shape, jnp.int32),
            pltpu.VMEM(jump_rows.shape, jnp.int32),
            pltpu.SMEM(counts.shape, jnp.int32),
            pltpu.VMEM(contact.shape, jnp.int32),
            pltpu.VMEM((width, width), F32),
            pltpu.VMEM((width, width), BF16),
            pltpu.VMEM((width, width), BF16),
            pltpu.VMEM((width, lanes), BF16),
            pltpu.VMEM((width, lanes + 2 * FACE), BF16),
            pltpu.VMEM((width, lanes + 2 * FACE), BF16),
            pltpu.VMEM((plans, halves + 1, 1, 128), F32),
            pltpu.VMEM((plans, halves, 1, 128), F32),
            pltpu.VMEM((plans, halves + 1, 1, 128), F32),
            pltpu.VMEM((2, plans, halves, 1, 128), F32),
            pltpu.VMEM((2, loads, FACE), F32),
            pltpu.VMEM((2, loads, FACE), F32),
            pltpu.VMEM((2, 2, plans // PLANES, halves, 1, 128), F32),
            pltpu.VMEM((2, 8, FACE), F32),
            pltpu.VMEM((2, 8, FACE), F32),
            pltpu.VMEM((4, 1, 128), F32),
            pltpu.VMEM((2, total, 1, 128), F32),
            pltpu.VMEM((halves, 1, 128), F32),
            pltpu.VMEM((loads, lanes), F32),
            pltpu.VMEM((loads, lanes), F32),
            pltpu.VMEM((8, lanes), F32),
            pltpu.VMEM((8, lanes), F32),
            pltpu.VMEM((2, loads, FACE), F32),
            pltpu.VMEM((loads, lanes), F32),
            pltpu.VMEM((2, loads, FACE), F32),
            pltpu.VMEM((plans, halves, 1, 128), F32),
            pltpu.VMEM((plans, halves, 1, 128), F32),
            dma((6,)), dma((width // CHUNK,)),
            dma, dma, dma((2, PLANES)), dma((2,)), dma((plans // PLANES,)), dma((2, 2)),
            dma((2,)), dma((2,)), dma((2,)), dma((2,)),
            dma, dma((2,)),
            dma, dma((2,)),
        ],
        compiler_params=pltpu.CompilerParams(
            collective_id=0, has_side_effects=True, vmem_limit_bytes=67_000_000
        ),
        name="dual_steps",
    )(dual_block, start, load, partners, jump_rows, counts, contact)
    return both[:1], both[1:]


def solution(mesh):
    block = P("layer", "plan", None, None)
    in_specs = (
        block, block, block, P("plan", None), block, P("layer", "plan", None), P("layer", "plan", None),
    )
    body = functools.partial(shards, mesh.shape["plan"], mesh.shape["layer"])
    return jax.shard_map(
        body, mesh=mesh, in_specs=in_specs, out_specs=(block, block), check_vma=False
    )
```

```python
import functools

import jax
import jax.numpy as jnp
from jax import lax
from jax.experimental import pallas as pl
from jax.experimental.pallas import tpu as pltpu
from jax.sharding import PartitionSpec as P

FACE = 128
ITERS = 4
PLANES = 4
CHUNK = 256
MESH = pl.DeviceIdType.MESH
F32 = jnp.float32
BF16 = jnp.bfloat16


def split2(x):
    hi = x.astype(BF16)
    lo = (x - hi.astype(F32)).astype(BF16)
    return jnp.concatenate([hi, lo], axis=0)


def split3(x):
    hi = x.astype(BF16)
    rest = x - hi.astype(F32)
    mid = rest.astype(BF16)
    lo = (rest - mid.astype(F32)).astype(BF16)
    return jnp.concatenate([hi, mid, lo], axis=0)


def fold(y, parts):
    n = y.shape[0] // parts
    total = y[:n]
    for i in range(1, parts):
        total = total + y[i * n : (i + 1) * n]
    return total


def kernel(
    plans, layers, block_hbm, start_hbm, load_hbm, partners_hbm, rows_hbm, counts_hbm, contact_hbm,
    out_ref,
    start_ref, load_ref, partners_ref, rows_ref, counts_ref, contact_ref,
    block_f32, block_hi, block_lo, select, front_hi, front_lo,
    init_send, send_rows, init_rows, recv_rows, init_face, recv_face, meet, fcon_send, fcon_recv, ar_send, ar_recv,
    products, m_rows, h_rows, h_con, own_con, h_face, load_rows, face_send, flag_send, flag_rows,
    small_sem, block_sem, rows_send_sem, init_rows_sem, rows_recv_sem, init_face_sem, meet_send_sem, meet_sem,
    face_send_sem, face_recv_sem, fcon_send_sem, fcon_recv_sem, ar_send_sem, ar_recv_sem,
    init_send_sem, init_face_send_sem, flag_send_sem, flag_sem,
):
    out_m, out_g = out_ref.at[pl.ds(0, 1)], out_ref.at[pl.ds(1, 1)]
    rounds, jr = rows_ref.shape[0], rows_ref.shape[2]
    loads, width = start_ref.shape[2], start_ref.shape[3]
    lanes = plans * jr
    per = 128 // jr
    halves = loads // per
    tiles = lanes // 128
    total = plans * layers
    part_of = plans // PLANES
    plan = lax.axis_index("plan")
    layer = lax.axis_index("layer")
    me = plan * layers + layer

    plane = plan // part_of
    place = lax.rem(plan, part_of)
    near = part_of * layers
    spot = me - plane * near
    far = (PLANES - 1) * (1 - (2 * plane) // PLANES)
    second = lax.rem(2 + (PLANES - 1) * plane, PLANES + 1)
    third = 1 + lax.rem(plane, 2)
    at_end = plane % (PLANES - 1) == 0
    barrier = pltpu.get_barrier_semaphore()

    def greet(d_plan, d_layer):
        pl.semaphore_signal(
            barrier, inc=1, device_id={"plan": d_plan, "layer": d_layer}, device_id_type=MESH
        )

    def greet_plane(z, first):
        def body(o, c):
            greet(z * part_of + lax.rem(place + o, part_of), layer)
            return c

        lax.fori_loop(first, part_of, body, 0, unroll=True)

    for z in (far, second, third):
        greet_plane(z, 0)
    for o in range(1, layers):
        greet(plan, lax.rem(layer + o, layers))
    greet_plane(plane, 1)
    small = [
        pltpu.make_async_copy(src, dst, small_sem.at[i])
        for i, (src, dst) in enumerate((
            (rows_hbm, rows_ref), (partners_hbm, partners_ref), (counts_hbm, counts_ref),
            (start_hbm, start_ref), (contact_hbm, contact_ref), (load_hbm, load_ref),
        ))
    ]
    for copy in small:
        copy.start()
    chunks = width // CHUNK
    for c in range(chunks):
        pltpu.make_async_copy(
            block_hbm.at[0, 0, pl.ds(c * CHUNK, CHUNK)], block_f32.at[pl.ds(c * CHUNK, CHUNK)],
            block_sem.at[c],
        ).start()

    k_of = lax.broadcasted_iota(jnp.int32, (jr, lanes), 0)
    l_of = lax.broadcasted_iota(jnp.int32, (jr, lanes), 1)
    spread = jnp.where(lax.rem(l_of, jr) == k_of, 1.0, 0.0).astype(BF16)
    init_rows[plan] = jnp.zeros((halves, 1, 128), F32)
    flag_rows[plan] = jnp.zeros((1, 1, 128), F32)
    for s in range(2):
        recv_rows[s, plan] = jnp.zeros((halves, 1, 128), F32)

    @pl.when(layer == 0)
    def _():
        init_face[0] = jnp.zeros((loads, FACE), F32)
        recv_face[0] = jnp.zeros((loads, FACE), F32)
        fcon_recv[0] = jnp.zeros((8, FACE), F32)

    @pl.when(layer == layers - 1)
    def _():
        init_face[1] = jnp.zeros((loads, FACE), F32)
        recv_face[1] = jnp.zeros((loads, FACE), F32)
        fcon_recv[1] = jnp.zeros((8, FACE), F32)

    for s in range(2):
        ar_recv[s, me] = jnp.zeros((1, 128), F32)

    for copy in small[:3]:
        copy.wait()
    rows_f = jnp.concatenate([rows_ref[r] for r in range(rounds)], axis=0).astype(F32)
    r_hi = rows_f.astype(BF16)
    r_lo = (rows_f - r_hi.astype(F32)).astype(BF16)
    tiled = jnp.dot(r_hi, spread, preferred_element_type=F32) + jnp.dot(
        r_lo, spread, preferred_element_type=F32
    )
    lane = lax.broadcasted_iota(jnp.int32, (1, lanes), 1)
    lane_q = lane // jr
    lane_k = lax.rem(lane, jr)
    slot = jnp.full((1, lanes), -1.0, F32)
    for r in range(rounds):
        mine = (lane_q == partners_ref[0, r]) & (lane_k < counts_ref[0, 0, r])
        slot = jnp.where(mine, tiled[r : r + 1], slot)
    for c in range(width // 128):
        ids = lax.broadcasted_iota(jnp.int32, (128, lanes), 0).astype(F32) + float(c * 128)
        select[pl.ds(c * 128, 128), :] = jnp.where(ids == slot, 1.0, 0.0).astype(BF16)

    def gather(x):
        return fold(jnp.dot(split3(x), select[...], preferred_element_type=F32), 3)

    def scatter(x):
        y = lax.dot_general(
            split3(x), select[...], (((1,), (1,)), ((), ())), preferred_element_type=F32
        )
        return fold(y, 3)

    def times(xs, hi, lo):
        y = jnp.dot(xs, hi, preferred_element_type=F32) + jnp.dot(
            xs, lo, preferred_element_type=F32
        )
        return fold(y, 2)

    def matvec(x):
        return times(split2(x), block_hi[...], block_lo[...])

    def pick(dst, src):
        def body(c, carry):
            part = pl.ds(pl.multiple_of(c * CHUNK, CHUNK), CHUNK)
            a = jnp.dot(src[part, :], select[...], preferred_element_type=F32)
            dst[part, :lanes] = a.astype(BF16)
            dst[part, lanes : lanes + FACE] = src[part, :FACE]
            dst[part, lanes + FACE :] = src[part, width - FACE :]
            return carry

        lax.fori_loop(0, chunks, body, 0)

    sub_id = lax.broadcasted_iota(jnp.int32, (loads, 128), 0)
    group_id = lax.broadcasted_iota(jnp.int32, (loads, 128), 1) // jr

    def swap(x):
        b = 1
        while b < per:
            sb = lax.rem(sub_id // b, 2)
            gb = lax.rem(group_id // b, 2)
            down = pltpu.roll(pltpu.roll(x, b, 0), 128 - b * jr, 1)
            up = pltpu.roll(pltpu.roll(x, loads - b, 0), b * jr, 1)
            x = jnp.where(sb == gb, x, jnp.where(sb == 1, down, up))
            b *= 2
        return x

    def put_rows(x, dst):
        for j in range(tiles):
            t = swap(x[:, j * 128 : (j + 1) * 128])
            for g in range(per):
                for a in range(halves):
                    dst[j * per + g, a] = t[a * per + g : a * per + g + 1]

    def get_rows(src):
        parts = []
        for j in range(tiles):
            t = [src[j * per + g, a] for a in range(halves) for g in range(per)]
            parts.append(swap(jnp.concatenate(t, axis=0)))
        return jnp.concatenate(parts, axis=1)

    def rows_copy(src, dst, send_sem, recv_sem):
        def copy(z, o):
            q = z * part_of + lax.rem(place + o, part_of)
            return pltpu.make_async_remote_copy(
                src.at[q], dst.at[plan], send_sem, recv_sem,
                device_id={"plan": q, "layer": layer}, device_id_type=MESH,
            )

        return copy

    def start_plane(copy, z, first, n):
        def body(o, c):
            copy(z, o).start()
            return c

        lax.fori_loop(first, n, body, 0, unroll=True)

    def start_rows(copy):
        for z in (far, second, third):
            start_plane(copy, z, 0, part_of)
        start_plane(copy, plane, 1, part_of)

    def drain(ref, n, sem):
        whole = ref.at[pl.ds(0, n)]
        pltpu.make_async_copy(whole, whole, sem).wait()

    def face_copies(src, dst, send_sem, recv_sem, first, last):
        up = pltpu.make_async_remote_copy(
            last(src), dst.at[0], send_sem.at[0], recv_sem.at[0],
            device_id={"plan": plan, "layer": lax.rem(layer + 1, layers)}, device_id_type=MESH,
        )
        down = pltpu.make_async_remote_copy(
            first(src), dst.at[1], send_sem.at[1], recv_sem.at[1],
            device_id={"plan": plan, "layer": lax.rem(layer + layers - 1, layers)}, device_id_type=MESH,
        )
        return up, down

    has_up = layer < layers - 1
    has_down = layer > 0

    def face_start(copies):
        up, down = copies

        @pl.when(has_up)
        def _():
            up.start()

        @pl.when(has_down)
        def _():
            down.start()

    def face_wait(copies):
        up, down = copies

        @pl.when(has_up)
        def _():
            up.wait_send()
            down.wait_recv()

        @pl.when(has_down)
        def _():
            down.wait_send()
            up.wait_recv()

    def get_flags(src):
        mine = lax.rem(plan, per)
        parts = []
        for j in range(tiles):
            acc = jnp.zeros((8, 128), F32)
            for g in range(per):
                shift = lax.rem(g + per - mine, per) * jr
                row = jnp.broadcast_to(src[j * per + g, 0], (8, 128))
                acc = jnp.where(group_id == g, pltpu.roll(row, shift, 1), acc)
            parts.append(acc)
        return jnp.concatenate(parts, axis=1)

    def meet_copy(s, end, there, w):
        low, high = (place, w) if end == 0 else (w, place)
        q = part_of + (high // 2) * 2 + lax.rem(low, 2)
        slot = (low // 2) * 2 + lax.rem(high, 2)
        return pltpu.make_async_remote_copy(
            send_rows.at[there * part_of + w], meet.at[s, 0 if end == 0 else 1, slot],
            meet_send_sem.at[w], meet_sem.at[s, 0 if end == 0 else 1],
            device_id={"plan": q, "layer": layer}, device_id_type=MESH,
        )

    small[3].wait()
    start_m = start_ref[0, 0]
    mr0 = gather(start_m)
    m_rows[...] = mr0
    out_m[0, 0] = start_m
    put_rows(mr0, init_send)
    pl.semaphore_wait(barrier, plans - 1 + layers - 1)

    m_faces = face_copies(
        start_ref, init_face, init_face_send_sem, init_face_sem,
        lambda r: r.at[0, 0, :, pl.ds(0, FACE)], lambda r: r.at[0, 0, :, pl.ds(width - FACE, FACE)],
    )
    c_faces = face_copies(
        fcon_send, fcon_recv, fcon_send_sem, fcon_recv_sem, lambda r: r.at[0], lambda r: r.at[1]
    )
    g_faces = face_copies(
        face_send, recv_face, face_send_sem, face_recv_sem, lambda r: r.at[0], lambda r: r.at[1]
    )
    start_rows(rows_copy(init_send, init_rows, init_send_sem, init_rows_sem))
    face_start(m_faces)

    xs = split2(start_m)
    y = None
    for c in range(chunks):
        part = pl.ds(c * CHUNK, CHUNK)
        pltpu.make_async_copy(block_hbm.at[0, 0, part], block_f32.at[part], block_sem.at[c]).wait()
        a = block_f32[part, :]
        hi = a.astype(BF16)
        lo = (a - hi.astype(F32)).astype(BF16)
        block_hi[part, :] = hi
        block_lo[part, :] = lo
        xc = xs[:, c * CHUNK : (c + 1) * CHUNK]
        t = jnp.dot(xc, hi, preferred_element_type=F32) + jnp.dot(xc, lo, preferred_element_type=F32)
        y = t if y is None else y + t
    small[5].wait()
    load = load_ref[0, 0]
    base = fold(y, 2) - load
    base_r = gather(base)
    put_rows(base_r, send_rows)
    face_send[0] = base[:, :FACE]
    face_send[1] = base[:, width - FACE :]
    start_rows(rows_copy(send_rows, recv_rows.at[0], rows_send_sem, rows_recv_sem.at[0, plane]))
    face_start(g_faces)
    small[4].wait()
    con = jnp.where(contact_ref[0] == 1, 1.0, 0.0)
    flags = jnp.dot(
        jnp.broadcast_to(con, (16, width)).astype(BF16), select[...], preferred_element_type=F32
    )[:8]
    own_con[...] = flags
    for q in range(plans):
        j = q // per
        flag_send[q, 0] = flags[:1, j * 128 : (j + 1) * 128]
    fcon_send[0] = jnp.broadcast_to(con[:, :FACE], (8, FACE))
    fcon_send[1] = jnp.broadcast_to(con[:, width - FACE :], (8, FACE))
    start_rows(rows_copy(flag_send, flag_rows, flag_send_sem, flag_sem))
    face_start(c_faces)

    pick(front_hi, block_hi)
    drain(init_rows, plans - 1, init_rows_sem)
    face_wait(m_faces)

    sub = lax.broadcasted_iota(jnp.int32, (loads, 128), 0)
    ln = lax.broadcasted_iota(jnp.int32, (loads, 128), 1)
    contact_all = jnp.broadcast_to(con, (loads, width)) > 0.5

    def folded(x):
        t = x[:, :128]
        for j in range(1, x.shape[1] // 128):
            t = t + x[:, j * 128 : (j + 1) * 128]
        return t

    def local_sums(g, gr):
        ga = matvec(g)
        gs = jnp.sum(g * g, axis=1, keepdims=True)
        g_lo = g[:, :FACE]
        g_hi = g[:, width - FACE :]
        curved = folded(g * ga) + folded(gr * gr) + (g_lo * g_lo + g_hi * g_hi)
        return jnp.where(ln == sub, gs, 0.0), curved

    def sums_start(s, squares, curved, left, right, meets):
        def products_of(z):
            acc = jnp.zeros((halves, 1, 128), F32)
            for w in range(part_of):
                q = z * part_of + w
                acc = acc + left(q) * right(q)
            return acc

        def arrive(z, n):
            drain(recv_rows.at[s], n, rows_recv_sem.at[s, z])

        def message(slot, shared_rows):
            shared = jnp.zeros((loads, 128), F32)
            for a in range(halves):
                row = jnp.broadcast_to(shared_rows[a], (loads, 128))
                shared = jnp.where(sub_id // per == a, row, shared)
            shared = jnp.where(group_id == lax.rem(sub_id, per), shared, 0.0)
            cv = jnp.sum(curved - shared, axis=1, keepdims=True)
            mine = jnp.where(ln == sub + loads, cv, squares)
            ar_send[slot] = jnp.sum(mine, axis=0, keepdims=True)

        def send(slot, z, first=0):
            def copy(z, o):
                d = z * near + lax.rem(spot + o, near)
                return pltpu.make_async_remote_copy(
                    ar_send.at[slot], ar_recv.at[s, me], ar_send_sem, ar_recv_sem.at[s],
                    device_id={"plan": d // layers, "layer": lax.rem(d, layers)}, device_id_type=MESH,
                )

            start_plane(copy, z, first, near)

        arrive(plane, part_of - 1)
        own = products_of(plane)

        @pl.when(at_end)
        def _():
            message(1, own)
            send(1, far)
            send(1, second)
            if meets:
                send(1, third)
            arrive(third, part_of)
            arrive(second, part_of)
            some = own + 2.0 * (products_of(third) + products_of(second))
            arrive(far, part_of)
            last = 2.0 * products_of(far)
            message(0, some + last)
            if not meets:
                message(2, own + last)
            send(0, plane, 1)
            if not meets:
                send(2, third)

        @pl.when(jnp.logical_not(at_end))
        def _():
            arrive(second, part_of)
            one = own + 2.0 * products_of(second)
            message(1, one)
            send(1, far)
            arrive(third, part_of)
            other = 2.0 * products_of(third)
            arrive(far, part_of)
            last = 2.0 * products_of(far)
            products[...] = jnp.zeros((halves, 1, 128), F32)
            if meets:

                @pl.when(plane == 1)
                def _():
                    drain(meet.at[s, 0], part_of, meet_sem.at[s, 0])
                    drain(meet.at[s, 1], part_of, meet_sem.at[s, 1])
                    acc = jnp.zeros((halves, 1, 128), F32)
                    for w in range(part_of):
                        acc = acc + meet[s, 0, w] * meet[s, 1, w]
                    products[...] = 2.0 * acc

            met = products[...]
            message(2, one + last + met)
            message(3, own + other + last)
            message(0, one + other + last + met)
            send(2, third)
            send(3, second)
            send(0, plane, 1)

    def sums_end(s):
        drain(ar_recv.at[s], total - 1, ar_recv_sem.at[s])
        sums = ar_send[0] + jnp.sum(ar_recv[s], axis=0)
        sums = jnp.broadcast_to(sums, (loads, 128))
        num = jnp.sum(jnp.where(ln == sub, sums, 0.0), axis=1, keepdims=True)
        den = jnp.sum(jnp.where(ln == sub + loads, sums, 0.0), axis=1, keepdims=True)
        drain(ar_recv.at[s], total - 1, ar_send_sem)
        return (num + 1e-6) / (den + 1e-6)

    def move_all(alpha, m, g, mr, gr, hm, hg, below, above):
        def move(x, grad, flag):
            moved = x - alpha * grad
            return jnp.where(flag, jnp.maximum(moved, 0.0), moved)

        out_m[0, 0] = move(m, g, contact_all)
        m_rows[...] = move(mr, gr, own_con[...] > 0.5)
        h_rows[...] = move(hm, hg, h_con[...] > 0.5)
        h_face[0] = move(h_face[0], below, fcon_recv[0] > 0.5)
        h_face[1] = move(h_face[1], above, fcon_recv[1] > 0.5)

    hm0 = get_rows(init_rows)
    apart = mr0 - hm0
    low_apart = start_m[:, :FACE] - init_face[0]
    high_apart = start_m[:, width - FACE :] - init_face[1]
    h_face[0] = init_face[0]
    h_face[1] = init_face[1]
    gr0 = base_r + apart
    g0 = base + scatter(apart)
    g0 = jnp.concatenate(
        [g0[:, :FACE] + low_apart, g0[:, FACE : width - FACE], g0[:, width - FACE :] + high_apart], axis=1
    )
    out_g[0, 0] = g0
    squares0, curved0 = local_sums(g0, gr0)
    face_wait(g_faces)
    below0 = jnp.where(has_down, recv_face[0] - low_apart, 0.0)
    above0 = jnp.where(has_up, recv_face[1] - high_apart, 0.0)
    curved0 = curved0 - (g0[:, :FACE] * below0 + g0[:, width - FACE :] * above0)

    def apart_of(q):
        return init_send[q] - init_rows[q]

    sums_start(
        0, squares0, curved0, lambda q: send_rows[q] + apart_of(q), lambda q: recv_rows[0, q] - apart_of(q), False
    )
    drain(flag_rows, plans - 1, flag_sem)
    h_con[...] = get_flags(flag_rows)
    face_wait(c_faces)
    hg0 = get_rows(recv_rows.at[0]) - apart
    pick(front_lo, block_lo)
    load_rows[...] = gather(load)
    drain(recv_rows.at[0], plans - 1, rows_send_sem)
    drain(init_rows, plans - 1, init_send_sem)
    drain(flag_rows, plans - 1, flag_send_sem)
    alpha0 = sums_end(0)
    move_all(alpha0, start_m, g0, mr0, gr0, hm0, hg0, below0, above0)

    def step(it, carry):
        m = out_m[0, 0]
        mr = m_rows[...]
        hm = h_rows[...]
        load = load_ref[0, 0]
        s = lax.rem(it, 2)
        apart = mr - hm
        xs = split2(m)
        gr = times(xs, front_hi[:, :lanes], front_lo[:, :lanes]) + (apart - load_rows[...])
        put_rows(gr, send_rows)
        ends = times(xs, front_hi[:, lanes:], front_lo[:, lanes:])
        g_lo = ends[:, :FACE] + (m[:, :FACE] - h_face[0]) - load[:, :FACE]
        g_hi = ends[:, FACE:] + (m[:, width - FACE :] - h_face[1]) - load[:, width - FACE :]
        face_send[0] = g_lo
        face_send[1] = g_hi
        face_start(g_faces)
        rows = rows_copy(send_rows, recv_rows.at[s], rows_send_sem, rows_recv_sem.at[s, plane])
        start_plane(rows, plane, 1, part_of)
        start_plane(rows, far, 0, part_of)
        for end, there in ((0, PLANES - 1), (PLANES - 1, 0)):

            @pl.when(plane == end)
            def _(end=end, there=there):
                for w in range(part_of):
                    meet_copy(s, end, there, w).start()

        start_plane(rows, second, 0, part_of)
        start_plane(rows, third, 0, part_of)
        inner = pl.ds(FACE, width - 2 * FACE)
        mid = times(xs, block_hi[:, inner], block_lo[:, inner])
        mid = mid + scatter(apart)[:, FACE : width - FACE] - load[:, FACE : width - FACE]
        g = jnp.concatenate([g_lo, mid, g_hi], axis=1)
        out_g[0, 0] = g
        squares, curved = local_sums(g, gr)
        face_wait(g_faces)
        below = recv_face[0]
        above = recv_face[1]
        curved = curved - (g_lo * below + g_hi * above)
        came = recv_rows.at[s]
        sums_start(s, squares, curved, lambda q: send_rows[q], lambda q: came[q], True)

        @pl.when(at_end)
        def _():
            for w in range(part_of):
                meet_copy(s, 0, PLANES - 1, w).wait_send()

        drain(came, plans - 1, rows_send_sem)
        hg = get_rows(came)
        alpha = sums_end(s)
        move_all(alpha, m, g, mr, gr, hm, hg, below, above)
        return carry

    lax.fori_loop(1, ITERS, step, 0)


def shards(plans, layers, dual_block, start, load, partners, jump_rows, counts, contact):
    loads, width = start.shape[2], start.shape[3]
    jr = jump_rows.shape[3]
    lanes = plans * jr
    halves = loads * jr // 128
    jump_rows = jump_rows.reshape(jump_rows.shape[2], 1, jr)
    total = plans * layers
    vmem = pl.BlockSpec(memory_space=pltpu.VMEM)
    dma = pltpu.SemaphoreType.DMA
    out = jax.ShapeDtypeStruct((2, 1, loads, width), F32)
    both = pl.pallas_call(
        functools.partial(kernel, plans, layers),
        out_shape=out,
        in_specs=[pl.BlockSpec(memory_space=pl.ANY)] * 7,
        out_specs=vmem,
        scratch_shapes=[
            pltpu.VMEM(start.shape, F32),
            pltpu.VMEM(load.shape, F32),
            pltpu.SMEM(partners.shape, jnp.int32),
            pltpu.VMEM(jump_rows.shape, jnp.int32),
            pltpu.SMEM(counts.shape, jnp.int32),
            pltpu.VMEM(contact.shape, jnp.int32),
            pltpu.VMEM((width, width), F32),
            pltpu.VMEM((width, width), BF16),
            pltpu.VMEM((width, width), BF16),
            pltpu.VMEM((width, lanes), BF16),
            pltpu.VMEM((width, lanes + 2 * FACE), BF16),
            pltpu.VMEM((width, lanes + 2 * FACE), BF16),
            pltpu.VMEM((plans, halves, 1, 128), F32),
            pltpu.VMEM((plans, halves, 1, 128), F32),
            pltpu.VMEM((plans, halves, 1, 128), F32),
            pltpu.VMEM((2, plans, halves, 1, 128), F32),
            pltpu.VMEM((2, loads, FACE), F32),
            pltpu.VMEM((2, loads, FACE), F32),
            pltpu.VMEM((2, 2, plans // PLANES, halves, 1, 128), F32),
            pltpu.VMEM((2, 8, FACE), F32),
            pltpu.VMEM((2, 8, FACE), F32),
            pltpu.VMEM((4, 1, 128), F32),
            pltpu.VMEM((2, total, 1, 128), F32),
            pltpu.VMEM((halves, 1, 128), F32),
            pltpu.VMEM((loads, lanes), F32),
            pltpu.VMEM((loads, lanes), F32),
            pltpu.VMEM((8, lanes), F32),
            pltpu.VMEM((8, lanes), F32),
            pltpu.VMEM((2, loads, FACE), F32),
            pltpu.VMEM((loads, lanes), F32),
            pltpu.VMEM((2, loads, FACE), F32),
            pltpu.VMEM((plans, 1, 1, 128), F32),
            pltpu.VMEM((plans, 1, 1, 128), F32),
            dma((6,)), dma((width // CHUNK,)),
            dma, dma, dma((2, PLANES)), dma((2,)), dma((plans // PLANES,)), dma((2, 2)),
            dma((2,)), dma((2,)), dma((2,)), dma((2,)),
            dma, dma((2,)),
            dma, dma((2,)),
            dma, dma,
        ],
        compiler_params=pltpu.CompilerParams(
            collective_id=0, has_side_effects=True, vmem_limit_bytes=67_000_000
        ),
        name="dual_steps",
    )(dual_block, start, load, partners, jump_rows, counts, contact)
    return both[:1], both[1:]


def solution(mesh):
    block = P("layer", "plan", None, None)
    in_specs = (
        block, block, block, P("plan", None), block, P("layer", "plan", None), P("layer", "plan", None),
    )
    body = functools.partial(shards, mesh.shape["plan"], mesh.shape["layer"])
    return jax.shard_map(
        body, mesh=mesh, in_specs=in_specs, out_specs=(block, block), check_vma=False
    )
```

```python
import functools

import jax
import jax.numpy as jnp
from jax import lax
from jax.experimental import pallas as pl
from jax.experimental.pallas import tpu as pltpu
from jax.sharding import PartitionSpec as P

FACE = 128
ITERS = 4
PLANES = 4
CHUNK = 256
MESH = pl.DeviceIdType.MESH
F32 = jnp.float32
BF16 = jnp.bfloat16


def split2(x):
    hi = x.astype(BF16)
    lo = (x - hi.astype(F32)).astype(BF16)
    return jnp.concatenate([hi, lo], axis=0)


def split3(x):
    hi = x.astype(BF16)
    rest = x - hi.astype(F32)
    mid = rest.astype(BF16)
    lo = (rest - mid.astype(F32)).astype(BF16)
    return jnp.concatenate([hi, mid, lo], axis=0)


def fold(y, parts):
    n = y.shape[0] // parts
    total = y[:n]
    for i in range(1, parts):
        total = total + y[i * n : (i + 1) * n]
    return total


def kernel(
    plans, layers, block_hbm, start_hbm, load_hbm, partners_hbm, rows_hbm, counts_hbm, contact_hbm,
    out_ref,
    start_ref, load_ref, partners_ref, rows_ref, counts_ref, contact_ref,
    block_f32, block_hi, block_lo, select, front_hi, front_lo,
    init_send, send_rows, init_rows, recv_rows, init_face, recv_face, meet, fcon_send, fcon_recv, ar_send, ar_recv,
    products, m_rows, h_rows, h_con, own_con, h_face, load_rows, face_send, flag_send, flag_rows,
    small_sem, block_sem, rows_send_sem, init_rows_sem, rows_recv_sem, init_face_sem, meet_send_sem, meet_sem,
    face_send_sem, face_recv_sem, fcon_send_sem, fcon_recv_sem, ar_send_sem, ar_recv_sem,
    init_send_sem, init_face_send_sem, flag_send_sem, flag_sem,
):
    out_m, out_g = out_ref.at[pl.ds(0, 1)], out_ref.at[pl.ds(1, 1)]
    rounds, jr = rows_ref.shape[0], rows_ref.shape[2]
    loads, width = start_ref.shape[2], start_ref.shape[3]
    lanes = plans * jr
    per = 128 // jr
    halves = loads // per
    tiles = lanes // 128
    total = plans * layers
    part_of = plans // PLANES
    plan = lax.axis_index("plan")
    layer = lax.axis_index("layer")
    me = plan * layers + layer

    plane = plan // part_of
    place = lax.rem(plan, part_of)
    near = part_of * layers
    spot = me - plane * near
    far = (PLANES - 1) * (1 - (2 * plane) // PLANES)
    second = lax.rem(2 + (PLANES - 1) * plane, PLANES + 1)
    third = 1 + lax.rem(plane, 2)
    at_end = plane % (PLANES - 1) == 0
    barrier = pltpu.get_barrier_semaphore()

    def greet(d_plan, d_layer):
        pl.semaphore_signal(
            barrier, inc=1, device_id={"plan": d_plan, "layer": d_layer}, device_id_type=MESH
        )

    def greet_plane(z, first):
        def body(o, c):
            greet(z * part_of + lax.rem(place + o, part_of), layer)
            return c

        lax.fori_loop(first, part_of, body, 0, unroll=True)

    for z in (far, second, third):
        greet_plane(z, 0)
    for o in range(1, layers):
        greet(plan, lax.rem(layer + o, layers))
    greet_plane(plane, 1)
    small = [
        pltpu.make_async_copy(src, dst, small_sem.at[i])
        for i, (src, dst) in enumerate((
            (rows_hbm, rows_ref), (partners_hbm, partners_ref), (counts_hbm, counts_ref),
            (start_hbm, start_ref), (contact_hbm, contact_ref), (load_hbm, load_ref),
        ))
    ]
    for copy in small:
        copy.start()
    chunks = width // CHUNK
    for c in range(chunks):
        pltpu.make_async_copy(
            block_hbm.at[0, 0, pl.ds(c * CHUNK, CHUNK)], block_f32.at[pl.ds(c * CHUNK, CHUNK)],
            block_sem.at[c],
        ).start()

    k_of = lax.broadcasted_iota(jnp.int32, (jr, lanes), 0)
    l_of = lax.broadcasted_iota(jnp.int32, (jr, lanes), 1)
    spread = jnp.where(lax.rem(l_of, jr) == k_of, 1.0, 0.0).astype(BF16)
    init_rows[plan] = jnp.zeros((halves, 1, 128), F32)
    flag_rows[plan] = jnp.zeros((1, 1, 128), F32)
    for s in range(2):
        recv_rows[s, plan] = jnp.zeros((halves, 1, 128), F32)

    @pl.when(layer == 0)
    def _():
        init_face[0] = jnp.zeros((loads, FACE), F32)
        recv_face[0] = jnp.zeros((loads, FACE), F32)
        fcon_recv[0] = jnp.zeros((8, FACE), F32)

    @pl.when(layer == layers - 1)
    def _():
        init_face[1] = jnp.zeros((loads, FACE), F32)
        recv_face[1] = jnp.zeros((loads, FACE), F32)
        fcon_recv[1] = jnp.zeros((8, FACE), F32)

    for s in range(2):
        ar_recv[s, me] = jnp.zeros((1, 128), F32)

    for copy in small[:3]:
        copy.wait()
    rows_f = jnp.concatenate([rows_ref[r] for r in range(rounds)], axis=0).astype(F32)
    r_hi = rows_f.astype(BF16)
    r_lo = (rows_f - r_hi.astype(F32)).astype(BF16)
    tiled = jnp.dot(r_hi, spread, preferred_element_type=F32) + jnp.dot(
        r_lo, spread, preferred_element_type=F32
    )
    lane = lax.broadcasted_iota(jnp.int32, (1, lanes), 1)
    lane_q = lane // jr
    lane_k = lax.rem(lane, jr)
    slot = jnp.full((1, lanes), -1.0, F32)
    for r in range(rounds):
        mine = (lane_q == partners_ref[0, r]) & (lane_k < counts_ref[0, 0, r])
        slot = jnp.where(mine, tiled[r : r + 1], slot)
    for c in range(width // 128):
        ids = lax.broadcasted_iota(jnp.int32, (128, lanes), 0).astype(F32) + float(c * 128)
        select[pl.ds(c * 128, 128), :] = jnp.where(ids == slot, 1.0, 0.0).astype(BF16)

    def gather(x):
        return fold(jnp.dot(split3(x), select[...], preferred_element_type=F32), 3)

    def scatter(x):
        y = lax.dot_general(
            split3(x), select[...], (((1,), (1,)), ((), ())), preferred_element_type=F32
        )
        return fold(y, 3)

    def times(xs, hi, lo):
        y = jnp.dot(xs, hi, preferred_element_type=F32) + jnp.dot(
            xs, lo, preferred_element_type=F32
        )
        return fold(y, 2)

    def matvec(x):
        return times(split2(x), block_hi[...], block_lo[...])

    def pick(dst, src, first, last):
        def body(c, carry):
            part = pl.ds(pl.multiple_of(c * CHUNK, CHUNK), CHUNK)
            a = jnp.dot(src[part, :], select[...], preferred_element_type=F32)
            dst[part, :lanes] = a.astype(BF16)
            dst[part, lanes : lanes + FACE] = src[part, :FACE]
            dst[part, lanes + FACE :] = src[part, width - FACE :]
            return carry

        lax.fori_loop(first, last, body, 0)

    sub_id = lax.broadcasted_iota(jnp.int32, (loads, 128), 0)
    group_id = lax.broadcasted_iota(jnp.int32, (loads, 128), 1) // jr

    def swap(x):
        b = 1
        while b < per:
            sb = lax.rem(sub_id // b, 2)
            gb = lax.rem(group_id // b, 2)
            down = pltpu.roll(pltpu.roll(x, b, 0), 128 - b * jr, 1)
            up = pltpu.roll(pltpu.roll(x, loads - b, 0), b * jr, 1)
            x = jnp.where(sb == gb, x, jnp.where(sb == 1, down, up))
            b *= 2
        return x

    def put_rows(x, dst):
        for j in range(tiles):
            t = swap(x[:, j * 128 : (j + 1) * 128])
            for g in range(per):
                for a in range(halves):
                    dst[j * per + g, a] = t[a * per + g : a * per + g + 1]

    def get_rows(src):
        parts = []
        for j in range(tiles):
            t = [src[j * per + g, a] for a in range(halves) for g in range(per)]
            parts.append(swap(jnp.concatenate(t, axis=0)))
        return jnp.concatenate(parts, axis=1)

    def rows_copy(src, dst, send_sem, recv_sem):
        def copy(z, o):
            q = z * part_of + lax.rem(place + o, part_of)
            return pltpu.make_async_remote_copy(
                src.at[q], dst.at[plan], send_sem, recv_sem,
                device_id={"plan": q, "layer": layer}, device_id_type=MESH,
            )

        return copy

    def start_plane(copy, z, first, n):
        def body(o, c):
            copy(z, o).start()
            return c

        lax.fori_loop(first, n, body, 0, unroll=True)

    def start_rows(copy):
        for z in (far, second, third):
            start_plane(copy, z, 0, part_of)
        start_plane(copy, plane, 1, part_of)

    def drain(ref, n, sem):
        whole = ref.at[pl.ds(0, n)]
        pltpu.make_async_copy(whole, whole, sem).wait()

    def face_copies(src, dst, send_sem, recv_sem, first, last):
        up = pltpu.make_async_remote_copy(
            last(src), dst.at[0], send_sem.at[0], recv_sem.at[0],
            device_id={"plan": plan, "layer": lax.rem(layer + 1, layers)}, device_id_type=MESH,
        )
        down = pltpu.make_async_remote_copy(
            first(src), dst.at[1], send_sem.at[1], recv_sem.at[1],
            device_id={"plan": plan, "layer": lax.rem(layer + layers - 1, layers)}, device_id_type=MESH,
        )
        return up, down

    has_up = layer < layers - 1
    has_down = layer > 0

    def face_start(copies):
        up, down = copies

        @pl.when(has_up)
        def _():
            up.start()

        @pl.when(has_down)
        def _():
            down.start()

    def face_wait(copies):
        up, down = copies

        @pl.when(has_up)
        def _():
            up.wait_send()
            down.wait_recv()

        @pl.when(has_down)
        def _():
            down.wait_send()
            up.wait_recv()

    def get_flags(src):
        mine = lax.rem(plan, per)
        parts = []
        for j in range(tiles):
            acc = jnp.zeros((8, 128), F32)
            for g in range(per):
                shift = lax.rem(g + per - mine, per) * jr
                row = jnp.broadcast_to(src[j * per + g, 0], (8, 128))
                acc = jnp.where(group_id == g, pltpu.roll(row, shift, 1), acc)
            parts.append(acc)
        return jnp.concatenate(parts, axis=1)

    def meet_copy(s, end, there, w):
        low, high = (place, w) if end == 0 else (w, place)
        q = part_of + (high // 2) * 2 + lax.rem(low, 2)
        slot = (low // 2) * 2 + lax.rem(high, 2)
        return pltpu.make_async_remote_copy(
            send_rows.at[there * part_of + w], meet.at[s, 0 if end == 0 else 1, slot],
            meet_send_sem.at[w], meet_sem.at[s, 0 if end == 0 else 1],
            device_id={"plan": q, "layer": layer}, device_id_type=MESH,
        )

    small[3].wait()
    start_m = start_ref[0, 0]
    mr0 = gather(start_m)
    m_rows[...] = mr0
    out_m[0, 0] = start_m
    put_rows(mr0, init_send)
    pl.semaphore_wait(barrier, plans - 1 + layers - 1)

    m_faces = face_copies(
        start_ref, init_face, init_face_send_sem, init_face_sem,
        lambda r: r.at[0, 0, :, pl.ds(0, FACE)], lambda r: r.at[0, 0, :, pl.ds(width - FACE, FACE)],
    )
    c_faces = face_copies(
        fcon_send, fcon_recv, fcon_send_sem, fcon_recv_sem, lambda r: r.at[0], lambda r: r.at[1]
    )
    g_faces = face_copies(
        face_send, recv_face, face_send_sem, face_recv_sem, lambda r: r.at[0], lambda r: r.at[1]
    )
    start_rows(rows_copy(init_send, init_rows, init_send_sem, init_rows_sem))
    face_start(m_faces)

    xs = split2(start_m)
    y = None
    for c in range(chunks):
        part = pl.ds(c * CHUNK, CHUNK)
        pltpu.make_async_copy(block_hbm.at[0, 0, part], block_f32.at[part], block_sem.at[c]).wait()
        a = block_f32[part, :]
        hi = a.astype(BF16)
        lo = (a - hi.astype(F32)).astype(BF16)
        block_hi[part, :] = hi
        block_lo[part, :] = lo
        xc = xs[:, c * CHUNK : (c + 1) * CHUNK]
        t = jnp.dot(xc, hi, preferred_element_type=F32) + jnp.dot(xc, lo, preferred_element_type=F32)
        y = t if y is None else y + t
    small[5].wait()
    load = load_ref[0, 0]
    base = fold(y, 2) - load
    base_r = gather(base)
    put_rows(base_r, send_rows)
    face_send[0] = base[:, :FACE]
    face_send[1] = base[:, width - FACE :]
    start_rows(rows_copy(send_rows, recv_rows.at[0], rows_send_sem, rows_recv_sem.at[0, plane]))
    face_start(g_faces)
    small[4].wait()
    con = jnp.where(contact_ref[0] == 1, 1.0, 0.0)
    flags = jnp.dot(
        jnp.broadcast_to(con, (16, width)).astype(BF16), select[...], preferred_element_type=F32
    )[:8]
    own_con[...] = flags
    for q in range(plans):
        j = q // per
        flag_send[q, 0] = flags[:1, j * 128 : (j + 1) * 128]
    fcon_send[0] = jnp.broadcast_to(con[:, :FACE], (8, FACE))
    fcon_send[1] = jnp.broadcast_to(con[:, width - FACE :], (8, FACE))
    start_rows(rows_copy(flag_send, flag_rows, flag_send_sem, flag_sem))
    face_start(c_faces)

    pick(front_hi, block_hi, 0, chunks // 2)
    drain(init_rows, plans - 1, init_rows_sem)
    face_wait(m_faces)

    sub = lax.broadcasted_iota(jnp.int32, (loads, 128), 0)
    ln = lax.broadcasted_iota(jnp.int32, (loads, 128), 1)
    contact_all = jnp.broadcast_to(con, (loads, width)) > 0.5

    def folded(x):
        t = x[:, :128]
        for j in range(1, x.shape[1] // 128):
            t = t + x[:, j * 128 : (j + 1) * 128]
        return t

    def local_sums(g, gr):
        ga = matvec(g)
        gs = jnp.sum(g * g, axis=1, keepdims=True)
        g_lo = g[:, :FACE]
        g_hi = g[:, width - FACE :]
        curved = folded(g * ga) + folded(gr * gr) + (g_lo * g_lo + g_hi * g_hi)
        return jnp.where(ln == sub, gs, 0.0), curved

    def sums_start(s, squares, curved, left, right, meets):
        def products_of(z):
            acc = jnp.zeros((halves, 1, 128), F32)
            for w in range(part_of):
                q = z * part_of + w
                acc = acc + left(q) * right(q)
            return acc

        def arrive(z, n):
            drain(recv_rows.at[s], n, rows_recv_sem.at[s, z])

        def message(slot, shared_rows):
            shared = jnp.zeros((loads, 128), F32)
            for a in range(halves):
                row = jnp.broadcast_to(shared_rows[a], (loads, 128))
                shared = jnp.where(sub_id // per == a, row, shared)
            shared = jnp.where(group_id == lax.rem(sub_id, per), shared, 0.0)
            cv = jnp.sum(curved - shared, axis=1, keepdims=True)
            mine = jnp.where(ln == sub + loads, cv, squares)
            ar_send[slot] = jnp.sum(mine, axis=0, keepdims=True)

        def send(slot, z, first=0):
            def copy(z, o):
                d = z * near + lax.rem(spot + o, near)
                return pltpu.make_async_remote_copy(
                    ar_send.at[slot], ar_recv.at[s, me], ar_send_sem, ar_recv_sem.at[s],
                    device_id={"plan": d // layers, "layer": lax.rem(d, layers)}, device_id_type=MESH,
                )

            start_plane(copy, z, first, near)

        arrive(plane, part_of - 1)
        own = products_of(plane)

        @pl.when(at_end)
        def _():
            message(1, own)
            send(1, far)
            send(1, second)
            if meets:
                send(1, third)
            arrive(third, part_of)
            arrive(second, part_of)
            some = own + 2.0 * (products_of(third) + products_of(second))
            arrive(far, part_of)
            last = 2.0 * products_of(far)
            message(0, some + last)
            if not meets:
                message(2, own + last)
            send(0, plane, 1)
            if not meets:
                send(2, third)

        @pl.when(jnp.logical_not(at_end))
        def _():
            arrive(second, part_of)
            one = own + 2.0 * products_of(second)
            message(1, one)
            send(1, far)
            arrive(third, part_of)
            other = 2.0 * products_of(third)
            arrive(far, part_of)
            last = 2.0 * products_of(far)
            products[...] = jnp.zeros((halves, 1, 128), F32)
            if meets:

                @pl.when(plane == 1)
                def _():
                    drain(meet.at[s, 0], part_of, meet_sem.at[s, 0])
                    drain(meet.at[s, 1], part_of, meet_sem.at[s, 1])
                    acc = jnp.zeros((halves, 1, 128), F32)
                    for w in range(part_of):
                        acc = acc + meet[s, 0, w] * meet[s, 1, w]
                    products[...] = 2.0 * acc

            met = products[...]
            message(2, one + last + met)
            message(3, own + other + last)
            message(0, one + other + last + met)
            send(2, third)
            send(3, second)
            send(0, plane, 1)

    def sums_end(s):
        drain(ar_recv.at[s], total - 1, ar_recv_sem.at[s])
        sums = ar_send[0] + jnp.sum(ar_recv[s], axis=0)
        sums = jnp.broadcast_to(sums, (loads, 128))
        num = jnp.sum(jnp.where(ln == sub, sums, 0.0), axis=1, keepdims=True)
        den = jnp.sum(jnp.where(ln == sub + loads, sums, 0.0), axis=1, keepdims=True)
        drain(ar_recv.at[s], total - 1, ar_send_sem)
        return (num + 1e-6) / (den + 1e-6)

    def move_all(alpha, m, g, mr, gr, hm, hg, below, above):
        def move(x, grad, flag):
            moved = x - alpha * grad
            return jnp.where(flag, jnp.maximum(moved, 0.0), moved)

        out_m[0, 0] = move(m, g, contact_all)
        m_rows[...] = move(mr, gr, own_con[...] > 0.5)
        h_rows[...] = move(hm, hg, h_con[...] > 0.5)
        h_face[0] = move(h_face[0], below, fcon_recv[0] > 0.5)
        h_face[1] = move(h_face[1], above, fcon_recv[1] > 0.5)

    hm0 = get_rows(init_rows)
    apart = mr0 - hm0
    low_apart = start_m[:, :FACE] - init_face[0]
    high_apart = start_m[:, width - FACE :] - init_face[1]
    h_face[0] = init_face[0]
    h_face[1] = init_face[1]
    gr0 = base_r + apart
    g0 = base + scatter(apart)
    g0 = jnp.concatenate(
        [g0[:, :FACE] + low_apart, g0[:, FACE : width - FACE], g0[:, width - FACE :] + high_apart], axis=1
    )
    out_g[0, 0] = g0
    squares0, curved0 = local_sums(g0, gr0)
    face_wait(g_faces)
    below0 = jnp.where(has_down, recv_face[0] - low_apart, 0.0)
    above0 = jnp.where(has_up, recv_face[1] - high_apart, 0.0)
    curved0 = curved0 - (g0[:, :FACE] * below0 + g0[:, width - FACE :] * above0)

    def apart_of(q):
        return init_send[q] - init_rows[q]

    sums_start(
        0, squares0, curved0, lambda q: send_rows[q] + apart_of(q), lambda q: recv_rows[0, q] - apart_of(q), False
    )
    drain(flag_rows, plans - 1, flag_sem)
    h_con[...] = get_flags(flag_rows)
    face_wait(c_faces)
    hg0 = get_rows(recv_rows.at[0]) - apart
    pick(front_hi, block_hi, chunks // 2, chunks)
    pick(front_lo, block_lo, 0, chunks)
    load_rows[...] = gather(load)
    drain(recv_rows.at[0], plans - 1, rows_send_sem)
    drain(init_rows, plans - 1, init_send_sem)
    drain(flag_rows, plans - 1, flag_send_sem)
    alpha0 = sums_end(0)
    move_all(alpha0, start_m, g0, mr0, gr0, hm0, hg0, below0, above0)

    def step(it, carry):
        m = out_m[0, 0]
        mr = m_rows[...]
        hm = h_rows[...]
        load = load_ref[0, 0]
        s = lax.rem(it, 2)
        apart = mr - hm
        xs = split2(m)
        gr = times(xs, front_hi[:, :lanes], front_lo[:, :lanes]) + (apart - load_rows[...])
        put_rows(gr, send_rows)
        ends = times(xs, front_hi[:, lanes:], front_lo[:, lanes:])
        g_lo = ends[:, :FACE] + (m[:, :FACE] - h_face[0]) - load[:, :FACE]
        g_hi = ends[:, FACE:] + (m[:, width - FACE :] - h_face[1]) - load[:, width - FACE :]
        face_send[0] = g_lo
        face_send[1] = g_hi
        face_start(g_faces)
        rows = rows_copy(send_rows, recv_rows.at[s], rows_send_sem, rows_recv_sem.at[s, plane])
        start_plane(rows, plane, 1, part_of)
        start_plane(rows, far, 0, part_of)
        for end, there in ((0, PLANES - 1), (PLANES - 1, 0)):

            @pl.when(plane == end)
            def _(end=end, there=there):
                for w in range(part_of):
                    meet_copy(s, end, there, w).start()

        start_plane(rows, second, 0, part_of)
        start_plane(rows, third, 0, part_of)
        inner = pl.ds(FACE, width - 2 * FACE)
        mid = times(xs, block_hi[:, inner], block_lo[:, inner])
        mid = mid + scatter(apart)[:, FACE : width - FACE] - load[:, FACE : width - FACE]
        g = jnp.concatenate([g_lo, mid, g_hi], axis=1)
        out_g[0, 0] = g
        squares, curved = local_sums(g, gr)
        face_wait(g_faces)
        below = recv_face[0]
        above = recv_face[1]
        curved = curved - (g_lo * below + g_hi * above)
        came = recv_rows.at[s]
        sums_start(s, squares, curved, lambda q: send_rows[q], lambda q: came[q], True)

        @pl.when(at_end)
        def _():
            for w in range(part_of):
                meet_copy(s, 0, PLANES - 1, w).wait_send()

        drain(came, plans - 1, rows_send_sem)
        hg = get_rows(came)
        alpha = sums_end(s)
        move_all(alpha, m, g, mr, gr, hm, hg, below, above)
        return carry

    lax.fori_loop(1, ITERS, step, 0)


def shards(plans, layers, dual_block, start, load, partners, jump_rows, counts, contact):
    loads, width = start.shape[2], start.shape[3]
    jr = jump_rows.shape[3]
    lanes = plans * jr
    halves = loads * jr // 128
    jump_rows = jump_rows.reshape(jump_rows.shape[2], 1, jr)
    total = plans * layers
    vmem = pl.BlockSpec(memory_space=pltpu.VMEM)
    dma = pltpu.SemaphoreType.DMA
    out = jax.ShapeDtypeStruct((2, 1, loads, width), F32)
    both = pl.pallas_call(
        functools.partial(kernel, plans, layers),
        out_shape=out,
        in_specs=[pl.BlockSpec(memory_space=pl.ANY)] * 7,
        out_specs=vmem,
        scratch_shapes=[
            pltpu.VMEM(start.shape, F32),
            pltpu.VMEM(load.shape, F32),
            pltpu.SMEM(partners.shape, jnp.int32),
            pltpu.VMEM(jump_rows.shape, jnp.int32),
            pltpu.SMEM(counts.shape, jnp.int32),
            pltpu.VMEM(contact.shape, jnp.int32),
            pltpu.VMEM((width, width), F32),
            pltpu.VMEM((width, width), BF16),
            pltpu.VMEM((width, width), BF16),
            pltpu.VMEM((width, lanes), BF16),
            pltpu.VMEM((width, lanes + 2 * FACE), BF16),
            pltpu.VMEM((width, lanes + 2 * FACE), BF16),
            pltpu.VMEM((plans, halves, 1, 128), F32),
            pltpu.VMEM((plans, halves, 1, 128), F32),
            pltpu.VMEM((plans, halves, 1, 128), F32),
            pltpu.VMEM((2, plans, halves, 1, 128), F32),
            pltpu.VMEM((2, loads, FACE), F32),
            pltpu.VMEM((2, loads, FACE), F32),
            pltpu.VMEM((2, 2, plans // PLANES, halves, 1, 128), F32),
            pltpu.VMEM((2, 8, FACE), F32),
            pltpu.VMEM((2, 8, FACE), F32),
            pltpu.VMEM((4, 1, 128), F32),
            pltpu.VMEM((2, total, 1, 128), F32),
            pltpu.VMEM((halves, 1, 128), F32),
            pltpu.VMEM((loads, lanes), F32),
            pltpu.VMEM((loads, lanes), F32),
            pltpu.VMEM((8, lanes), F32),
            pltpu.VMEM((8, lanes), F32),
            pltpu.VMEM((2, loads, FACE), F32),
            pltpu.VMEM((loads, lanes), F32),
            pltpu.VMEM((2, loads, FACE), F32),
            pltpu.VMEM((plans, 1, 1, 128), F32),
            pltpu.VMEM((plans, 1, 1, 128), F32),
            dma((6,)), dma((width // CHUNK,)),
            dma, dma, dma((2, PLANES)), dma((2,)), dma((plans // PLANES,)), dma((2, 2)),
            dma((2,)), dma((2,)), dma((2,)), dma((2,)),
            dma, dma((2,)),
            dma, dma((2,)),
            dma, dma,
        ],
        compiler_params=pltpu.CompilerParams(
            collective_id=0, has_side_effects=True, vmem_limit_bytes=67_000_000
        ),
        name="dual_steps",
    )(dual_block, start, load, partners, jump_rows, counts, contact)
    return both[:1], both[1:]


def solution(mesh):
    block = P("layer", "plan", None, None)
    in_specs = (
        block, block, block, P("plan", None), block, P("layer", "plan", None), P("layer", "plan", None),
    )
    body = functools.partial(shards, mesh.shape["plan"], mesh.shape["layer"])
    return jax.shard_map(
        body, mesh=mesh, in_specs=in_specs, out_specs=(block, block), check_vma=False
    )
```
